128 devices in a mesh: dp: 8 (over y, core), ctx: 16 (over z, x).
Axes of the slice: x: 4, y: 4, z: 4, core: 2. Of those that a mesh axis runs over, the one named last changes fastest.
Arguments:
- queries: bfloat16 [8, 4096, 256], P('dp', 'ctx'), may hold values from -6 to 6
- keys: bfloat16 [8, 4096, 256], P('dp', 'ctx'), may hold values from -6 to 6
- values: bfloat16 [8, 4096, 256], P('dp', 'ctx'), may hold values from -6 to 6
- grad_out: bfloat16 [8, 4096, 256], P('dp', 'ctx'), may hold values from -6 to 6
- log_norm: float32 [8, 2, 4096], P('dp', None, 'ctx'), may hold values from 5 to 7
- offsets: int32 [2, 5], replicated, may hold values from 0 to 15
- q_gain: float32 [256], replicated, may hold values from 0.5 to 2
Outputs:
- grad_queries: bfloat16 [8, 4096, 256], P('dp', 'ctx')
- grad_keys: bfloat16 [8, 4096, 256], P('dp', 'ctx')
- grad_values: bfloat16 [8, 4096, 256], P('dp', 'ctx')
- grad_gain: float32 [256], replicated
The draws below stay inside these ranges and needn't reach their ends.
All inputs are finite; a program needn't handle non-finite values.
Results may differ from the reference program's by a relative error of at most 0.013.
The reference program's roundings to bfloat16 on the way (of `scaled`, `probs_low` and `dscore`) count: a program that leaves them out, or rounds other values in their place, can miss the bound.
Values may be sent and summed in bfloat16 or wider, within the bound.
No kernel may reach another device: no remote copies, remote signals or barrier semaphores. Data moves between devices by JAX's collectives and lax.ppermute only.
A program may use at most 64 MiB of HBM per device.

```python
import math
import jax
import jax.numpy as jnp
from jax import lax

HD = 128
HEADS_W = 2
HW = 256
BLOCK = 128
LEVELS = 5
TOK_DEV = 256
SEQ_LEN = 4096
SEQS = 8
N_CTX = 16


def touch_ends(drawn, rng, low, top_value):
    spot = [jax.random.randint(jax.random.fold_in(rng, axis), (), 0, length) for axis, length in enumerate(drawn.shape)]
    widest = drawn.shape.index(max(drawn.shape))
    beside = spot[:widest] + [(spot[widest] + 1) % drawn.shape[widest]] + spot[widest + 1:]
    return drawn.at[tuple(spot)].set(low).at[tuple(beside)].set(top_value)


def block_levels(stream_key, shape, split, least, high):
    level, own = 1.0, jax.random.fold_in(stream_key, 6)
    for axis_at, shards_of in split:
        heights = jnp.exp(jax.random.uniform(jax.random.fold_in(own, axis_at), (shards_of,), jnp.float32, least / len(split), high / len(split)))
        level = level * jnp.repeat(heights, shape[axis_at] // shards_of).reshape([-1 if axis == axis_at else 1 for axis in range(len(shape))])
    return level


def scatter_about(rng, dims, scale, most, split=(), kind=jnp.bfloat16):
    array = jax.random.normal(rng, dims, jnp.float32) * scale
    if len(split) > 0:
        array = block_levels(rng, dims, split, -0.22, 0.18) * array
    return jnp.clip(array, min=-most, max=most).astype(kind)


def setup_inputs(seed: int = 0) -> dict:
    arg_keys = jax.random.split(jax.random.key(seed), 8)
    return {
        "queries": scatter_about(arg_keys[0], (SEQS, SEQ_LEN, HW), 1.0, 6.0, ((0, 8), (1, 16))),
        "keys": scatter_about(arg_keys[1], (SEQS, SEQ_LEN, HW), 1.0, 6.0, ((0, 8), (1, 16))),
        "values": scatter_about(arg_keys[2], (SEQS, SEQ_LEN, HW), 1.0, 6.0, ((0, 8), (1, 16))),
        "grad_out": scatter_about(arg_keys[3], (SEQS, SEQ_LEN, HW), 1.0, 6.0, ((0, 8), (1, 16))),
        "log_norm": jnp.clip(5.0 + 2.0 * jax.random.uniform(arg_keys[4], (SEQS, HEADS_W, SEQ_LEN), jnp.float32) ** block_levels(arg_keys[4], (SEQS, HEADS_W, SEQ_LEN), ((0, 8), (2, 16)), -0.2, 0.2), 5.0, 7.0),
        "offsets": touch_ends(jax.random.randint(arg_keys[5], (HEADS_W, LEVELS), 0, N_CTX), jax.random.fold_in(arg_keys[5], 1), 0, N_CTX - 1).astype(jnp.int32),
        "q_gain": jnp.clip(jnp.exp(jax.random.uniform(arg_keys[6], (HW,), jnp.float32, math.log(0.5), math.log(2.0))), 0.5, 2.0),
    }


def group_grads(parts):
    query_rows, key_rows, value_rows, dout_rows, norm_rows = parts
    score_scale = HD ** -0.5
    scores = jnp.dot(query_rows, key_rows.T, preferred_element_type=jnp.float32) * score_scale
    probs = jnp.exp(scores - norm_rows[:, None])
    probs_low = lax.optimization_barrier(probs.astype(jnp.bfloat16))
    prob_grad = jnp.dot(dout_rows, value_rows.T, preferred_element_type=jnp.float32)
    dscore = lax.optimization_barrier((probs * prob_grad).astype(jnp.bfloat16))
    query_grad = jnp.dot(dscore, key_rows, preferred_element_type=jnp.float32) * score_scale
    key_grad = jnp.dot(dscore.T, query_rows, preferred_element_type=jnp.float32) * score_scale
    value_grad = jnp.dot(probs_low.T, dout_rows, preferred_element_type=jnp.float32)
    return query_grad, key_grad, value_grad


def reference(queries, keys, values, grad_out, log_norm, offsets, q_gain):
    seq_count, seq_len, proj_width = queries.shape
    scaled = (queries.astype(jnp.float32) * q_gain).astype(jnp.bfloat16)

    def by_head(matrix):
        return matrix.reshape(seq_count, seq_len, HEADS_W, HD).transpose(0, 2, 1, 3)

    query_field = by_head(scaled)
    key_field = by_head(keys)
    value_field = by_head(values)
    dout_field = by_head(grad_out)
    zero_field = jnp.zeros((seq_count, HEADS_W, seq_len, HD), jnp.float32)
    query_acc = zero_field
    key_acc = zero_field
    value_acc = zero_field
    block_dev = TOK_DEV // BLOCK
    for level_idx in range(LEVELS):
        span_len = min(2 ** level_idx, N_CTX)
        group_len = block_dev * span_len
        seg_count = seq_len // (group_len * BLOCK)
        for head_idx in range(HEADS_W):
            shift_val = (offsets[head_idx, level_idx] % span_len).astype(jnp.int32)
            chosen = (jnp.arange(seg_count, dtype=jnp.int32)[:, None] * group_len + shift_val
                      + span_len * jnp.arange(block_dev, dtype=jnp.int32)[None, :])
            token_idx = (chosen[:, :, None] * BLOCK + jnp.arange(BLOCK, dtype=jnp.int32)[None, None, :]).reshape(seg_count, TOK_DEV)
            picked = [field[:, head_idx][:, token_idx].reshape(seq_count * seg_count, TOK_DEV, HD)
                      for field in (query_field, key_field, value_field, dout_field)]
            norm_pick = log_norm[:, head_idx][:, token_idx].reshape(seq_count * seg_count, TOK_DEV)
            results = lax.map(group_grads, (picked[0], picked[1], picked[2], picked[3], norm_pick))
            shaped = [part.reshape(seq_count, seg_count, TOK_DEV, HD) for part in results]
            query_acc = query_acc.at[:, head_idx, token_idx].add(shaped[0])
            key_acc = key_acc.at[:, head_idx, token_idx].add(shaped[1])
            value_acc = value_acc.at[:, head_idx, token_idx].add(shaped[2])

    def rows_of(field_acc):
        return field_acc.transpose(0, 2, 1, 3).reshape(seq_count, seq_len, proj_width)

    dq_rows = rows_of(query_acc)
    grad_queries = (dq_rows * q_gain).astype(jnp.bfloat16)
    grad_gain = jnp.sum(queries.astype(jnp.float32) * dq_rows, axis=(0, 1))
    return (grad_queries, rows_of(key_acc).astype(jnp.bfloat16), rows_of(value_acc).astype(jnp.bfloat16), grad_gain)
```

```python
import functools

import jax
import jax.numpy as jnp
from jax import lax
from jax.experimental import pallas as pl
from jax.experimental.pallas import tpu as pltpu
from jax.sharding import PartitionSpec as P

BLOCK = 128
LEVELS = 5
HEADS = 2
HD = 128
SCALE = HD**-0.5
ROW_Q, ROW_K, ROW_V, ROW_D, ROW_N, ROWS = 0, 128, 256, 384, 512, 528

VMEM = pl.BlockSpec(memory_space=pltpu.VMEM)
SMEM = pl.BlockSpec(memory_space=pltpu.SMEM)
NT = (((1,), (1,)), ((), ()))
TN = (((0,), (0,)), ((), ()))
NN = (((1,), (0,)), ((), ()))


def dot(left, right, dims):
    return lax.dot_general(left, right, dims, preferred_element_type=jnp.float32)


def cols(head):
    return slice(head * HD, (head + 1) * HD)


def place(offsets, me, head, level):
    half = 1 << (level - 1)
    shift = offsets[head, level] & (2 * half - 1)
    return (me & (half - 1)) == (shift >> 1), shift & 1


def block_rows(block):
    return pl.ds(pl.multiple_of(block * BLOCK, BLOCK), BLOCK)


def scale_rows(rows, gain):
    return (rows.astype(jnp.float32) * gain).astype(jnp.bfloat16)


def pack_kernel(offsets, gain, q, k, v, d, norm, *outs):
    row = lax.broadcasted_iota(jnp.int32, (16, BLOCK), 0)
    for head in range(HEADS):
        for level in range(1, LEVELS):
            out = outs[level - 1]
            block = offsets[head, level] & 1
            at = block_rows(block)
            out[head, ROW_Q : ROW_Q + BLOCK] = scale_rows(q[at, cols(head)], gain[:, cols(head)])
            out[head, ROW_K : ROW_K + BLOCK] = k[at, cols(head)]
            out[head, ROW_V : ROW_V + BLOCK] = v[at, cols(head)]
            out[head, ROW_D : ROW_D + BLOCK] = d[at, cols(head)]
            whole = jnp.where(block == 0, norm[head : head + 1, :BLOCK], norm[head : head + 1, BLOCK:])
            high = whole.astype(jnp.bfloat16).astype(jnp.float32)
            rest = whole - high
            mid = rest.astype(jnp.bfloat16).astype(jnp.float32)
            low = rest - mid
            parts = jnp.where(row == 0, high, jnp.where(row == 1, mid, jnp.where(row == 2, low, 0.0)))
            out[head, ROW_N:ROWS] = parts.astype(jnp.bfloat16)


def local_kernel(offsets, gain, q, k, v, d, norm, dq, dk, dv, norm_cols):
    me = lax.axis_index("ctx")
    for head in range(HEADS):
        c = cols(head)
        count = [jnp.float32(1.0), jnp.float32(1.0)]
        for level in range(1, LEVELS):
            active, block = place(offsets, me, head, level)
            for b in range(2):
                count[b] = count[b] + jnp.where(active & (block == b), 1.0, 0.0)
        query, key, value, dout = scale_rows(q[:, c], gain[:, c]), k[:, c], v[:, c], d[:, c]
        probs = jnp.exp(dot(key, query, NT) * SCALE - norm[head : head + 1, :])
        grads = (probs * dot(value, dout, NT)).astype(jnp.bfloat16)
        probs = probs.astype(jnp.bfloat16)
        for b in range(2):
            own, other = slice(b * BLOCK, (b + 1) * BLOCK), slice((1 - b) * BLOCK, (2 - b) * BLOCK)
            dq[own, c] = count[b] * dot(grads[own, own], key[own], TN) + dot(grads[other, own], key[other], TN)
            dk[own, c] = count[b] * dot(grads[own, own], query[own], NN) + dot(grads[own, other], query[other], NN)
            dv[own, c] = count[b] * dot(probs[own, own], dout[own], NN) + dot(probs[own, other], dout[other], NN)
        norm_cols[head] = jnp.transpose(jnp.broadcast_to(norm[head : head + 1, :], (BLOCK, 2 * BLOCK)))


def for_each_level(offsets, fn):
    me = lax.axis_index("ctx")
    for level in range(1, LEVELS):
        spots = [place(offsets, me, head, level) for head in range(HEADS)]

        def both(level=level, spots=spots):
            fn(level, spots)

        if level == 1:
            both()
        else:
            pl.when(spots[0][0] | spots[1][0])(both)


def query_kernel(offsets, gain, q, d, norm_cols, dq_in, r1, r2, r3, r4, grad_q, partial, acc):
    received = (r1, r2, r3, r4)
    acc[...] = dq_in[...]

    def one(level, spots):
        got = received[level - 1]
        for head in range(HEADS):
            active, block = spots[head]
            c, at = cols(head), block_rows(block)
            query = scale_rows(q[at, c], gain[:, c])
            key, value = got[head, ROW_K : ROW_K + BLOCK], got[head, ROW_V : ROW_V + BLOCK]
            probs = jnp.exp(dot(query, key, NT) * SCALE - norm_cols[head, at, :])
            grads = (probs * dot(d[at, c], value, NT)).astype(jnp.bfloat16)
            acc[at, c] += jnp.where(active, dot(grads, key, NN), 0.0)

    for_each_level(offsets, one)
    total = acc[...] * SCALE
    grad_q[...] = (total * gain[...]).astype(jnp.bfloat16)
    partial[...] = jnp.sum(q[...].astype(jnp.float32) * total, axis=0, keepdims=True)


def key_kernel(offsets, k, v, dk_in, dv_in, r1, r2, r3, r4, grad_k, grad_v, dk, dv):
    received = (r1, r2, r3, r4)
    dk[...] = dk_in[...]
    dv[...] = dv_in[...]

    def one(level, spots):
        got = received[level - 1]
        for head in range(HEADS):
            active, block = spots[head]
            c, at = cols(head), block_rows(block)
            query, dout = got[head, ROW_Q : ROW_Q + BLOCK], got[head, ROW_D : ROW_D + BLOCK]
            parts = got[head, ROW_N:ROWS].astype(jnp.float32)
            norm = parts[0:1] + parts[1:2] + parts[2:3]
            probs = jnp.exp(dot(k[at, c], query, NT) * SCALE - norm)
            grads = (probs * dot(v[at, c], dout, NT)).astype(jnp.bfloat16)
            dk[at, c] += jnp.where(active, dot(grads, query, NN), 0.0)
            dv[at, c] += jnp.where(active, dot(probs.astype(jnp.bfloat16), dout, NN), 0.0)

    for_each_level(offsets, one)
    grad_k[...] = (dk[...] * SCALE).astype(jnp.bfloat16)
    grad_v[...] = dv[...].astype(jnp.bfloat16)


def call(kernel, name, outs, in_specs, scratch=()):
    return pl.pallas_call(
        kernel,
        name=name,
        out_shape=outs,
        in_specs=in_specs,
        out_specs=[VMEM] * len(outs),
        scratch_shapes=list(scratch),
        compiler_params=pltpu.CompilerParams(vmem_limit_bytes=32 * 1024 * 1024),
    )


def body(queries, keys, values, grad_out, log_norm, offsets, q_gain):
    q, k, v, d = queries[0], keys[0], values[0], grad_out[0]
    norm = log_norm[0]
    tokens, width = q.shape
    gain = q_gain.reshape(1, width)
    f32 = functools.partial(jax.ShapeDtypeStruct, dtype=jnp.float32)
    bf16 = functools.partial(jax.ShapeDtypeStruct, dtype=jnp.bfloat16)
    sent = call(pack_kernel, "pack", [bf16((HEADS, ROWS, HD))] * (LEVELS - 1), [SMEM] + [VMEM] * 6)(
        offsets, gain, q, k, v, d, norm
    )
    got = []
    for level in range(1, LEVELS):
        half = 1 << (level - 1)
        route = [(i, i ^ half) for i in range(lax.axis_size("ctx"))]
        got.append(lax.ppermute(sent[level - 1], "ctx", route))
    dq, dk, dv, norm_cols = call(
        local_kernel, "local", [f32((tokens, width))] * 3 + [f32((HEADS, tokens, HD))], [SMEM] + [VMEM] * 6
    )(offsets, gain, q, k, v, d, norm)
    acc = pltpu.VMEM((tokens, width), jnp.float32)
    grad_q, partial = call(
        query_kernel, "remote_q", [bf16((tokens, width)), f32((1, width))], [SMEM] + [VMEM] * 9, [acc]
    )(offsets, gain, q, d, norm_cols, dq, *got)
    axes = ("dp", "ctx")
    everyone = lax.axis_size(axes)
    parts = lax.all_to_all(jnp.broadcast_to(partial, (everyone, width)), axes, 0, 0, tiled=True)
    grad_k, grad_v = call(
        key_kernel, "remote_kv", [bf16((tokens, width))] * 2, [SMEM] + [VMEM] * 8, [acc, acc]
    )(offsets, k, v, dk, dv, *got)
    return (grad_q[None], grad_k[None], grad_v[None], jnp.sum(parts, axis=0))


def solution(mesh):
    rows = P("dp", "ctx", None)
    in_specs = (rows, rows, rows, rows, P("dp", None, "ctx"), P(), P())
    out_specs = (rows, rows, rows, P())
    return jax.shard_map(body, mesh=mesh, in_specs=in_specs, out_specs=out_specs, check_vma=False)
```

```python
import functools

import jax
import jax.numpy as jnp
from jax import lax
from jax.experimental import pallas as pl
from jax.experimental.pallas import tpu as pltpu
from jax.sharding import PartitionSpec as P

BLOCK = 128
LEVELS = 5
HEADS = 2
HD = 128
SCALE = HD**-0.5
ROW_Q, ROW_D, ROW_N, ROWS = 0, 128, 256, 272

HBM = pl.BlockSpec(memory_space=pltpu.HBM)
VMEM = pl.BlockSpec(memory_space=pltpu.VMEM)
SMEM = pl.BlockSpec(memory_space=pltpu.SMEM)
NT = (((1,), (1,)), ((), ()))
TN = (((0,), (0,)), ((), ()))
NN = (((1,), (0,)), ((), ()))


def dot(left, right, dims):
    return lax.dot_general(left, right, dims, preferred_element_type=jnp.float32)


def cols(head):
    return slice(head * HD, (head + 1) * HD)


def place(offsets, me, head, level):
    half = 1 << (level - 1)
    shift = offsets[head, level] & (2 * half - 1)
    return (me & (half - 1)) == (shift >> 1), shift & 1


def block_rows(block):
    return pl.ds(pl.multiple_of(block * BLOCK, BLOCK), BLOCK)


def scale_rows(rows, gain):
    return (rows.astype(jnp.float32) * gain).astype(jnp.bfloat16)


def copy_blocks(offsets, sources, outs, sems):
    copies = []
    for level in range(1, LEVELS):
        for head in range(HEADS):
            at = block_rows(offsets[head, level] & 1)
            for i, source in enumerate(sources):
                copies.append(
                    pltpu.make_async_copy(
                        source.at[at, cols(head)],
                        outs[level - 1].at[head, i * BLOCK : (i + 1) * BLOCK],
                        sems.at[level - 1, head, i],
                    )
                )
    for copy in copies:
        copy.start()
    return copies


def pack_kv_kernel(offsets, k, v, *refs):
    for copy in copy_blocks(offsets, (k, v), refs[:-1], refs[-1]):
        copy.wait()


def pack_qd_kernel(offsets, q, d, norm, *refs):
    outs, sems = refs[:-1], refs[-1]
    copies = copy_blocks(offsets, (q, d), outs, sems)
    row = lax.broadcasted_iota(jnp.int32, (16, BLOCK), 0)
    for head in range(HEADS):
        for level in range(1, LEVELS):
            block = offsets[head, level] & 1
            whole = jnp.where(block == 0, norm[head : head + 1, :BLOCK], norm[head : head + 1, BLOCK:])
            high = whole.astype(jnp.bfloat16).astype(jnp.float32)
            rest = whole - high
            mid = rest.astype(jnp.bfloat16).astype(jnp.float32)
            low = rest - mid
            parts = jnp.where(row == 0, high, jnp.where(row == 1, mid, jnp.where(row == 2, low, 0.0)))
            outs[level - 1][head, ROW_N:ROWS] = parts.astype(jnp.bfloat16)
    for copy in copies:
        copy.wait()


def local_kernel(offsets, gain, q, k, v, d, norm, dq, dk, dv, norm_cols, scaled):
    me = lax.axis_index("ctx")
    for head in range(HEADS):
        c = cols(head)
        count = [jnp.float32(1.0), jnp.float32(1.0)]
        for level in range(1, LEVELS):
            active, block = place(offsets, me, head, level)
            for b in range(2):
                count[b] = count[b] + jnp.where(active & (block == b), 1.0, 0.0)
        query, key, value, dout = scale_rows(q[:, c], gain[:, c]), k[:, c], v[:, c], d[:, c]
        scaled[:, c] = query
        probs = jnp.exp(dot(key, query, NT) * SCALE - norm[head : head + 1, :])
        grads = (probs * dot(value, dout, NT)).astype(jnp.bfloat16)
        probs = probs.astype(jnp.bfloat16)
        for b in range(2):
            own, other = slice(b * BLOCK, (b + 1) * BLOCK), slice((1 - b) * BLOCK, (2 - b) * BLOCK)
            dq[own, c] = count[b] * dot(grads[own, own], key[own], TN) + dot(grads[other, own], key[other], TN)
            dk[own, c] = count[b] * dot(grads[own, own], query[own], NN) + dot(grads[own, other], query[other], NN)
            dv[own, c] = count[b] * dot(probs[own, own], dout[own], NN) + dot(probs[own, other], dout[other], NN)
        norm_cols[head] = jnp.transpose(jnp.broadcast_to(norm[head : head + 1, :], (BLOCK, 2 * BLOCK)))


def for_each_level(offsets, fn):
    me = lax.axis_index("ctx")
    for level in range(1, LEVELS):
        spots = [place(offsets, me, head, level) for head in range(HEADS)]

        def both(level=level, spots=spots):
            fn(level, spots)

        if level == 1:
            both()
        else:
            pl.when(spots[0][0] | spots[1][0])(both)


def query_kernel(offsets, scaled, q, d, norm_cols, dq_in, r1, r2, r3, r4, dq, partial):
    received = (r1, r2, r3, r4)
    dq[...] = dq_in[...]

    def one(level, spots):
        got = received[level - 1]
        for head in range(HEADS):
            active, block = spots[head]
            c, at = cols(head), block_rows(block)
            key, value = got[head, :BLOCK], got[head, BLOCK:]
            probs = jnp.exp(dot(scaled[at, c], key, NT) * SCALE - norm_cols[head, at, :])
            grads = (probs * dot(d[at, c], value, NT)).astype(jnp.bfloat16)
            dq[at, c] += jnp.where(active, dot(grads, key, NN), 0.0)

    for_each_level(offsets, one)
    total = jnp.sum(q[...].astype(jnp.float32) * (dq[...] * SCALE), axis=0, keepdims=True)
    partial[...] = jnp.broadcast_to(total[None], partial.shape)


def key_kernel(offsets, gain, k, v, dq, dk_in, dv_in, r1, r2, r3, r4, grad_q, grad_k, grad_v, dk, dv):
    received = (r1, r2, r3, r4)
    dk[...] = dk_in[...]
    dv[...] = dv_in[...]
    grad_q[...] = (dq[...] * SCALE * gain[...]).astype(jnp.bfloat16)

    def one(level, spots):
        got = received[level - 1]
        for head in range(HEADS):
            active, block = spots[head]
            c, at = cols(head), block_rows(block)
            query = scale_rows(got[head, ROW_Q : ROW_Q + BLOCK], gain[:, c])
            dout = got[head, ROW_D : ROW_D + BLOCK]
            parts = got[head, ROW_N:ROWS].astype(jnp.float32)
            norm = parts[0:1] + parts[1:2] + parts[2:3]
            probs = jnp.exp(dot(k[at, c], query, NT) * SCALE - norm)
            grads = (probs * dot(v[at, c], dout, NT)).astype(jnp.bfloat16)
            dk[at, c] += jnp.where(active, dot(grads, query, NN), 0.0)
            dv[at, c] += jnp.where(active, dot(probs.astype(jnp.bfloat16), dout, NN), 0.0)

    for_each_level(offsets, one)
    grad_k[...] = (dk[...] * SCALE).astype(jnp.bfloat16)
    grad_v[...] = dv[...].astype(jnp.bfloat16)


def call(kernel, name, outs, in_specs, scratch=()):
    return pl.pallas_call(
        kernel,
        name=name,
        out_shape=outs,
        in_specs=in_specs,
        out_specs=[VMEM] * len(outs),
        scratch_shapes=list(scratch),
        compiler_params=pltpu.CompilerParams(vmem_limit_bytes=32 * 1024 * 1024),
    )


def swap(payloads):
    count = lax.axis_size("ctx")
    return [lax.ppermute(p, "ctx", [(i, i ^ (1 << n)) for i in range(count)]) for n, p in enumerate(payloads)]


def body(queries, keys, values, grad_out, log_norm, offsets, q_gain):
    q, k, v, d = queries[0], keys[0], values[0], grad_out[0]
    norm = log_norm[0]
    tokens, width = q.shape
    gain = q_gain.reshape(1, width)
    f32 = functools.partial(jax.ShapeDtypeStruct, dtype=jnp.float32)
    bf16 = functools.partial(jax.ShapeDtypeStruct, dtype=jnp.bfloat16)
    sems = pltpu.SemaphoreType.DMA((LEVELS - 1, HEADS, 2))
    sent = call(pack_kv_kernel, "pack_kv", [bf16((HEADS, 2 * BLOCK, HD))] * (LEVELS - 1), [SMEM, HBM, HBM], [sems])(
        offsets, k, v
    )
    got_kv = swap(sent)
    sent = call(pack_qd_kernel, "pack_qd", [bf16((HEADS, ROWS, HD))] * (LEVELS - 1), [SMEM, HBM, HBM, VMEM], [sems])(
        offsets, q, d, norm
    )
    got_qd = swap(sent)
    dq, dk, dv, norm_cols, scaled = call(
        local_kernel,
        "local",
        [f32((tokens, width))] * 3 + [f32((HEADS, tokens, HD)), bf16((tokens, width))],
        [SMEM] + [VMEM] * 6,
    )(offsets, gain, q, k, v, d, norm)
    axes = ("dp", "ctx")
    everyone = lax.axis_size(axes)
    dq, partial = call(
        query_kernel, "remote_q", [f32((tokens, width)), f32((everyone, 1, width))], [SMEM] + [VMEM] * 9
    )(offsets, scaled, q, d, norm_cols, dq, *got_kv)
    parts = lax.all_to_all(partial, axes, 0, 0, tiled=True)
    acc = pltpu.VMEM((tokens, width), jnp.float32)
    grad_q, grad_k, grad_v = call(
        key_kernel, "remote_kv", [bf16((tokens, width))] * 3, [SMEM] + [VMEM] * 10, [acc, acc]
    )(offsets, gain, k, v, dq, dk, dv, *got_qd)
    return (grad_q[None], grad_k[None], grad_v[None], jnp.sum(parts, axis=(0, 1)))


def solution(mesh):
    rows = P("dp", "ctx", None)
    in_specs = (rows, rows, rows, rows, P("dp", None, "ctx"), P(), P())
    out_specs = (rows, rows, rows, P())
    return jax.shard_map(body, mesh=mesh, in_specs=in_specs, out_specs=out_specs, check_vma=False)
```

```python
import functools

import jax
import jax.numpy as jnp
from jax import lax
from jax.experimental import pallas as pl
from jax.experimental.pallas import tpu as pltpu
from jax.sharding import PartitionSpec as P

BLOCK = 128
LEVELS = 5
HEADS = 2
HD = 128
SCALE = HD**-0.5
ROW_Q, ROW_D, ROW_N, ROWS = 0, 128, 256, 272

HBM = pl.BlockSpec(memory_space=pltpu.HBM)
VMEM = pl.BlockSpec(memory_space=pltpu.VMEM)
SMEM = pl.BlockSpec(memory_space=pltpu.SMEM)
NT = (((1,), (1,)), ((), ()))
TN = (((0,), (0,)), ((), ()))
NN = (((1,), (0,)), ((), ()))


def dot(left, right, dims):
    return lax.dot_general(left, right, dims, preferred_element_type=jnp.float32)


def cols(head):
    return slice(head * HD, (head + 1) * HD)


def place(offsets, me, head, level):
    half = 1 << (level - 1)
    shift = offsets[head, level] & (2 * half - 1)
    return (me & (half - 1)) == (shift >> 1), shift & 1


def block_rows(block):
    return pl.ds(pl.multiple_of(block * BLOCK, BLOCK), BLOCK)


def scale_rows(rows, gain):
    return (rows.astype(jnp.float32) * gain).astype(jnp.bfloat16)


def copy_blocks(offsets, sources, outs, sems):
    copies = []
    for level in range(1, LEVELS):
        for head in range(HEADS):
            at = block_rows(offsets[head, level] & 1)
            for i, source in enumerate(sources):
                copies.append(
                    pltpu.make_async_copy(
                        source.at[at, cols(head)],
                        outs[level - 1].at[head, i * BLOCK : (i + 1) * BLOCK],
                        sems.at[level - 1, head, i],
                    )
                )
    for copy in copies:
        copy.start()
    return copies


def pack_kv_kernel(offsets, k, v, *refs):
    for copy in copy_blocks(offsets, (k, v), refs[:-1], refs[-1]):
        copy.wait()


def pack_qd_kernel(offsets, q, d, norm, *refs):
    outs, sems = refs[:-1], refs[-1]
    copies = copy_blocks(offsets, (q, d), outs, sems)
    row = lax.broadcasted_iota(jnp.int32, (16, BLOCK), 0)
    for head in range(HEADS):
        for level in range(1, LEVELS):
            block = offsets[head, level] & 1
            whole = jnp.where(block == 0, norm[head : head + 1, :BLOCK], norm[head : head + 1, BLOCK:])
            high = whole.astype(jnp.bfloat16).astype(jnp.float32)
            rest = whole - high
            mid = rest.astype(jnp.bfloat16).astype(jnp.float32)
            low = rest - mid
            parts = jnp.where(row == 0, high, jnp.where(row == 1, mid, jnp.where(row == 2, low, 0.0)))
            outs[level - 1][head, ROW_N:ROWS] = parts.astype(jnp.bfloat16)
    for copy in copies:
        copy.wait()


def local_kernel(offsets, gain, q, k, v, d, norm, dq, dk, dv, norm_cols, scaled):
    me = lax.axis_index("ctx")
    for head in range(HEADS):
        c = cols(head)
        count = [jnp.float32(1.0), jnp.float32(1.0)]
        for level in range(1, LEVELS):
            active, block = place(offsets, me, head, level)
            for b in range(2):
                count[b] = count[b] + jnp.where(active & (block == b), 1.0, 0.0)
        query, key, value, dout = scale_rows(q[:, c], gain[:, c]), k[:, c], v[:, c], d[:, c]
        scaled[:, c] = query
        probs = jnp.exp(dot(key, query, NT) * SCALE - norm[head : head + 1, :])
        grads = (probs * dot(value, dout, NT)).astype(jnp.bfloat16)
        probs = probs.astype(jnp.bfloat16)
        for b in range(2):
            own, other = slice(b * BLOCK, (b + 1) * BLOCK), slice((1 - b) * BLOCK, (2 - b) * BLOCK)
            dq[own, c] = count[b] * dot(grads[own, own], key[own], TN) + dot(grads[other, own], key[other], TN)
            dk[own, c] = count[b] * dot(grads[own, own], query[own], NN) + dot(grads[own, other], query[other], NN)
            dv[own, c] = count[b] * dot(probs[own, own], dout[own], NN) + dot(probs[own, other], dout[other], NN)
        norm_cols[head] = jnp.transpose(jnp.broadcast_to(norm[head : head + 1, :], (BLOCK, 2 * BLOCK)))


def for_each_level(offsets, fn):
    me = lax.axis_index("ctx")
    for level in range(1, LEVELS):
        spots = [place(offsets, me, head, level) for head in range(HEADS)]

        def both(level=level, spots=spots):
            fn(level, spots)

        if level == 1:
            both()
        else:
            pl.when(spots[0][0] | spots[1][0])(both)


def query_kernel(offsets, scaled, q, d, norm_cols, dq_in, r1, r2, r3, r4, dq, partial):
    received = (r1, r2, r3, r4)
    dq[...] = dq_in[...]

    def one(level, spots):
        got = received[level - 1]
        for head in range(HEADS):
            active, block = spots[head]
            c, at = cols(head), block_rows(block)
            key, value = got[head, :BLOCK], got[head, BLOCK:]
            probs = jnp.exp(dot(scaled[at, c], key, NT) * SCALE - norm_cols[head, at, :])
            grads = (probs * dot(d[at, c], value, NT)).astype(jnp.bfloat16)
            dq[at, c] += jnp.where(active, dot(grads, key, NN), 0.0)

    for_each_level(offsets, one)
    total = jnp.sum(q[...].astype(jnp.float32) * (dq[...] * SCALE), axis=0, keepdims=True)
    partial[...] = jnp.broadcast_to(total[None], partial.shape)


def key_kernel(offsets, gain, k, v, dq, dk_in, dv_in, r1, r2, r3, r4, grad_q, grad_k, grad_v, dk, dv):
    received = (r1, r2, r3, r4)
    dk[...] = dk_in[...]
    dv[...] = dv_in[...]
    grad_q[...] = (dq[...] * SCALE * gain[...]).astype(jnp.bfloat16)

    def one(level, spots):
        got = received[level - 1]
        for head in range(HEADS):
            active, block = spots[head]
            c, at = cols(head), block_rows(block)
            query = scale_rows(got[head, ROW_Q : ROW_Q + BLOCK], gain[:, c])
            dout = got[head, ROW_D : ROW_D + BLOCK]
            parts = got[head, ROW_N:ROWS].astype(jnp.float32)
            norm = parts[0:1] + parts[1:2] + parts[2:3]
            probs = jnp.exp(dot(k[at, c], query, NT) * SCALE - norm)
            grads = (probs * dot(v[at, c], dout, NT)).astype(jnp.bfloat16)
            dk[at, c] += jnp.where(active, dot(grads, query, NN), 0.0)
            dv[at, c] += jnp.where(active, dot(probs.astype(jnp.bfloat16), dout, NN), 0.0)

    for_each_level(offsets, one)
    grad_k[...] = (dk[...] * SCALE).astype(jnp.bfloat16)
    grad_v[...] = dv[...].astype(jnp.bfloat16)


def call(kernel, name, outs, in_specs, scratch=()):
    return pl.pallas_call(
        kernel,
        name=name,
        out_shape=outs,
        in_specs=in_specs,
        out_specs=[VMEM] * len(outs),
        scratch_shapes=list(scratch),
        compiler_params=pltpu.CompilerParams(vmem_limit_bytes=32 * 1024 * 1024),
    )


def in_hbm(array):
    return pltpu.with_memory_space_constraint(array, pltpu.HBM)


def swap(payloads):
    count = lax.axis_size("ctx")
    return [lax.ppermute(p, "ctx", [(i, i ^ (1 << n)) for i in range(count)]) for n, p in enumerate(payloads)]


def body(queries, keys, values, grad_out, log_norm, offsets, q_gain):
    q, k, v, d = queries[0], keys[0], values[0], grad_out[0]
    norm = log_norm[0]
    tokens, width = q.shape
    gain = q_gain.reshape(1, width)
    f32 = functools.partial(jax.ShapeDtypeStruct, dtype=jnp.float32)
    bf16 = functools.partial(jax.ShapeDtypeStruct, dtype=jnp.bfloat16)
    sems = pltpu.SemaphoreType.DMA((LEVELS - 1, HEADS, 2))
    sent = call(pack_kv_kernel, "pack_kv", [bf16((HEADS, 2 * BLOCK, HD))] * (LEVELS - 1), [SMEM, HBM, HBM], [sems])(
        offsets, in_hbm(k), in_hbm(v)
    )
    got_kv = swap(sent)
    sent = call(pack_qd_kernel, "pack_qd", [bf16((HEADS, ROWS, HD))] * (LEVELS - 1), [SMEM, HBM, HBM, VMEM], [sems])(
        offsets, in_hbm(q), in_hbm(d), norm
    )
    got_qd = swap(sent)
    dq, dk, dv, norm_cols, scaled = call(
        local_kernel,
        "local",
        [f32((tokens, width))] * 3 + [f32((HEADS, tokens, HD)), bf16((tokens, width))],
        [SMEM] + [VMEM] * 6,
    )(offsets, gain, q, k, v, d, norm)
    axes = ("dp", "ctx")
    everyone = lax.axis_size(axes)
    dq, partial = call(
        query_kernel, "remote_q", [f32((tokens, width)), f32((everyone, 1, width))], [SMEM] + [VMEM] * 9
    )(offsets, scaled, q, d, norm_cols, dq, *got_kv)
    parts = lax.all_to_all(partial, axes, 0, 0, tiled=True)
    acc = pltpu.VMEM((tokens, width), jnp.float32)
    grad_q, grad_k, grad_v = call(
        key_kernel, "remote_kv", [bf16((tokens, width))] * 3, [SMEM] + [VMEM] * 10, [acc, acc]
    )(offsets, gain, k, v, dq, dk, dv, *got_qd)
    return (grad_q[None], grad_k[None], grad_v[None], jnp.sum(parts, axis=(0, 1)))


def solution(mesh):
    rows = P("dp", "ctx", None)
    in_specs = (rows, rows, rows, rows, P("dp", None, "ctx"), P(), P())
    out_specs = (rows, rows, rows, P())
    return jax.shard_map(body, mesh=mesh, in_specs=in_specs, out_specs=out_specs, check_vma=False)
```

```python
import functools

import jax
import jax.numpy as jnp
from jax import lax
from jax.experimental import pallas as pl
from jax.experimental.pallas import tpu as pltpu
from jax.sharding import PartitionSpec as P

BLOCK = 128
LEVELS = 5
HEADS = 2
HD = 128
SCALE = HD**-0.5
ROW_Q, ROW_D, ROW_N, ROWS = 0, 128, 256, 272

HBM = pl.BlockSpec(memory_space=pltpu.HBM)
ANY = pl.BlockSpec(memory_space=pl.ANY)
VMEM = pl.BlockSpec(memory_space=pltpu.VMEM)
SMEM = pl.BlockSpec(memory_space=pltpu.SMEM)
NT = (((1,), (1,)), ((), ()))
TN = (((0,), (0,)), ((), ()))
NN = (((1,), (0,)), ((), ()))


def dot(left, right, dims):
    return lax.dot_general(left, right, dims, preferred_element_type=jnp.float32)


def cols(head):
    return slice(head * HD, (head + 1) * HD)


def place(offsets, me, head, level):
    half = 1 << (level - 1)
    shift = offsets[head, level] & (2 * half - 1)
    return (me & (half - 1)) == (shift >> 1), shift & 1


def block_rows(block):
    return pl.ds(pl.multiple_of(block * BLOCK, BLOCK), BLOCK)


def scale_rows(rows, gain):
    return (rows.astype(jnp.float32) * gain).astype(jnp.bfloat16)


def pack_kernel(offsets_in, k_in, v_in, q_in, d_in, norm_in, *refs):
    outs, (offsets, k, v, q, d, norm, sems) = refs[:8], refs[8:]
    copies = []
    for i, (source, target) in enumerate(
        ((offsets_in, offsets), (k_in, k), (v_in, v), (q_in, q), (d_in, d), (norm_in, norm))
    ):
        copies.append(pltpu.make_async_copy(source, target, sems.at[i]))
        copies[-1].start()
    for copy in copies[:3]:
        copy.wait()
    spots = [(level, head, offsets[head, level] & 1) for level in range(1, LEVELS) for head in range(HEADS)]
    for level, head, block in spots:
        at, out = block_rows(block), outs[level - 1]
        out[head, :BLOCK] = k[at, cols(head)]
        out[head, BLOCK:] = v[at, cols(head)]
    for copy in copies[3:]:
        copy.wait()
    row = lax.broadcasted_iota(jnp.int32, (16, BLOCK), 0)
    for level, head, block in spots:
        at, out = block_rows(block), outs[LEVELS - 1 + level - 1]
        out[head, ROW_Q : ROW_Q + BLOCK] = q[at, cols(head)]
        out[head, ROW_D : ROW_D + BLOCK] = d[at, cols(head)]
        whole = jnp.where(block == 0, norm[head : head + 1, :BLOCK], norm[head : head + 1, BLOCK:])
        high = whole.astype(jnp.bfloat16).astype(jnp.float32)
        rest = whole - high
        mid = rest.astype(jnp.bfloat16).astype(jnp.float32)
        low = rest - mid
        parts = jnp.where(row == 0, high, jnp.where(row == 1, mid, jnp.where(row == 2, low, 0.0)))
        out[head, ROW_N:ROWS] = parts.astype(jnp.bfloat16)


def block_counts(offsets, head):
    me = lax.axis_index("ctx")
    count = [jnp.float32(1.0), jnp.float32(1.0)]
    for level in range(1, LEVELS):
        active, block = place(offsets, me, head, level)
        for b in range(2):
            count[b] = count[b] + jnp.where(active & (block == b), 1.0, 0.0)
    return count


def both_blocks(b):
    return slice(b * BLOCK, (b + 1) * BLOCK), slice((1 - b) * BLOCK, (2 - b) * BLOCK)


def local_q_kernel(offsets, gain, q, k, v, d, norm, dq, norm_cols, scaled):
    for head in range(HEADS):
        c = cols(head)
        count = block_counts(offsets, head)
        query, key, value, dout = scale_rows(q[:, c], gain[:, c]), k[:, c], v[:, c], d[:, c]
        scaled[:, c] = query
        column = jnp.transpose(jnp.broadcast_to(norm[head : head + 1, :], (BLOCK, 2 * BLOCK)))
        norm_cols[head] = column
        probs = jnp.exp(dot(query, key, NT) * SCALE - jnp.concatenate([column, column], axis=1))
        grads = (probs * dot(dout, value, NT)).astype(jnp.bfloat16)
        for b in range(2):
            own, other = both_blocks(b)
            dq[own, c] = count[b] * dot(grads[own, own], key[own], NN) + dot(grads[own, other], key[other], NN)


def local_kv_kernel(offsets, scaled, k, v, d, norm, dk, dv):
    for head in range(HEADS):
        c = cols(head)
        count = block_counts(offsets, head)
        query, key, value, dout = scaled[:, c], k[:, c], v[:, c], d[:, c]
        probs = jnp.exp(dot(key, query, NT) * SCALE - norm[head : head + 1, :])
        grads = (probs * dot(value, dout, NT)).astype(jnp.bfloat16)
        probs = probs.astype(jnp.bfloat16)
        for b in range(2):
            own, other = both_blocks(b)
            dk[own, c] = count[b] * dot(grads[own, own], query[own], NN) + dot(grads[own, other], query[other], NN)
            dv[own, c] = count[b] * dot(probs[own, own], dout[own], NN) + dot(probs[own, other], dout[other], NN)


def for_each_level(offsets, fn):
    me = lax.axis_index("ctx")
    for level in range(1, LEVELS):
        spots = [place(offsets, me, head, level) for head in range(HEADS)]

        def both(level=level, spots=spots):
            fn(level, spots)

        if level == 1:
            both()
        else:
            pl.when(spots[0][0] | spots[1][0])(both)


def query_kernel(offsets, scaled, q, d, norm_cols, dq_in, r1, r2, r3, r4, dq, partial):
    received = (r1, r2, r3, r4)
    dq[...] = dq_in[...]

    def one(level, spots):
        got = received[level - 1]
        for head in range(HEADS):
            active, block = spots[head]
            c, at = cols(head), block_rows(block)
            key, value = got[head, :BLOCK], got[head, BLOCK:]
            probs = jnp.exp(dot(scaled[at, c], key, NT) * SCALE - norm_cols[head, at, :])
            grads = (probs * dot(d[at, c], value, NT)).astype(jnp.bfloat16)
            dq[at, c] += jnp.where(active, dot(grads, key, NN), 0.0)

    for_each_level(offsets, one)
    total = jnp.sum(q[...].astype(jnp.float32) * (dq[...] * SCALE), axis=0, keepdims=True)
    partial[...] = jnp.broadcast_to(total[None], partial.shape)


def key_kernel(offsets, gain, k, v, dq, dk_in, dv_in, r1, r2, r3, r4, grad_q, grad_k, grad_v, dk, dv):
    received = (r1, r2, r3, r4)
    dk[...] = dk_in[...]
    dv[...] = dv_in[...]
    grad_q[...] = (dq[...] * SCALE * gain[...]).astype(jnp.bfloat16)

    def one(level, spots):
        got = received[level - 1]
        for head in range(HEADS):
            active, block = spots[head]
            c, at = cols(head), block_rows(block)
            query = scale_rows(got[head, ROW_Q : ROW_Q + BLOCK], gain[:, c])
            dout = got[head, ROW_D : ROW_D + BLOCK]
            parts = got[head, ROW_N:ROWS].astype(jnp.float32)
            norm = parts[0:1] + parts[1:2] + parts[2:3]
            probs = jnp.exp(dot(k[at, c], query, NT) * SCALE - norm)
            grads = (probs * dot(v[at, c], dout, NT)).astype(jnp.bfloat16)
            dk[at, c] += jnp.where(active, dot(grads, query, NN), 0.0)
            dv[at, c] += jnp.where(active, dot(probs.astype(jnp.bfloat16), dout, NN), 0.0)

    for_each_level(offsets, one)
    grad_k[...] = (dk[...] * SCALE).astype(jnp.bfloat16)
    grad_v[...] = dv[...].astype(jnp.bfloat16)


def call(kernel, name, outs, in_specs, scratch=(), out_specs=None, aliases=None):
    return pl.pallas_call(
        kernel,
        name=name,
        out_shape=outs,
        in_specs=in_specs,
        out_specs=out_specs or [VMEM] * len(outs),
        scratch_shapes=list(scratch),
        input_output_aliases=aliases or {},
        compiler_params=pltpu.CompilerParams(vmem_limit_bytes=32 * 1024 * 1024),
    )


def in_hbm(array):
    return pltpu.with_memory_space_constraint(array, pltpu.HBM)


def swap(payloads):
    count = lax.axis_size("ctx")
    return [lax.ppermute(p, "ctx", [(i, i ^ (1 << n)) for i in range(count)]) for n, p in enumerate(payloads)]


def body(queries, keys, values, grad_out, log_norm, offsets, q_gain):
    q, k, v, d = queries[0], keys[0], values[0], grad_out[0]
    norm = log_norm[0]
    tokens, width = q.shape
    gain = q_gain.reshape(1, width)
    f32 = functools.partial(jax.ShapeDtypeStruct, dtype=jnp.float32)
    bf16 = functools.partial(jax.ShapeDtypeStruct, dtype=jnp.bfloat16)
    many = LEVELS - 1
    raw = pltpu.VMEM((tokens, width), jnp.bfloat16)
    sent = call(
        pack_kernel,
        "pack",
        [bf16((HEADS, 2 * BLOCK, HD))] * many + [bf16((HEADS, ROWS, HD))] * many,
        [HBM] * 6,
        [
            pltpu.SMEM(offsets.shape, jnp.int32),
            raw,
            raw,
            raw,
            raw,
            pltpu.VMEM(norm.shape, jnp.float32),
            pltpu.SemaphoreType.DMA((6,)),
        ],
    )(*map(in_hbm, (offsets, k, v, q, d, norm)))
    got_kv, got_qd = swap(sent[:many]), swap(sent[many:])
    dq, norm_cols, scaled = call(
        local_q_kernel,
        "local_q",
        [f32((tokens, width)), f32((HEADS, tokens, HD)), bf16((tokens, width))],
        [SMEM] + [VMEM] * 6,
    )(offsets, gain, q, k, v, d, norm)
    axes = ("dp", "ctx")
    everyone = lax.axis_size(axes)
    dq, partial = call(
        query_kernel, "remote_q", [f32((tokens, width)), f32((everyone, 1, width))], [SMEM] + [VMEM] * 9
    )(offsets, scaled, q, d, norm_cols, dq, *got_kv)
    parts = lax.all_to_all(partial, axes, 0, 0, tiled=True)
    dk, dv = call(local_kv_kernel, "local_kv", [f32((tokens, width))] * 2, [SMEM] + [VMEM] * 5)(
        offsets, scaled, k, v, d, norm
    )
    acc = pltpu.VMEM((tokens, width), jnp.float32)
    grad_q, grad_k, grad_v = call(
        key_kernel, "remote_kv", [bf16((tokens, width))] * 3, [SMEM] + [VMEM] * 10, [acc, acc]
    )(offsets, gain, k, v, dq, dk, dv, *got_qd)
    return (grad_q[None], grad_k[None], grad_v[None], jnp.sum(parts, axis=(0, 1)))


def solution(mesh):
    rows = P("dp", "ctx", None)
    in_specs = (rows, rows, rows, rows, P("dp", None, "ctx"), P(), P())
    out_specs = (rows, rows, rows, P())
    return jax.shard_map(body, mesh=mesh, in_specs=in_specs, out_specs=out_specs, check_vma=False)
```

```python
import functools

import jax
import jax.numpy as jnp
from jax import lax
from jax.experimental import pallas as pl
from jax.experimental.pallas import tpu as pltpu
from jax.sharding import PartitionSpec as P

BLOCK = 128
LEVELS = 5
HEADS = 2
HD = 128
SCALE = HD**-0.5
EARLY = 16
PARTS, TAIL, FIRST, SECOND = 2 * BLOCK, 2 * BLOCK + 16, 2 * BLOCK + 16 + EARLY, 2 * BLOCK - EARLY

HBM = pl.BlockSpec(memory_space=pltpu.HBM)
ANY = pl.BlockSpec(memory_space=pl.ANY)
VMEM = pl.BlockSpec(memory_space=pltpu.VMEM)
SMEM = pl.BlockSpec(memory_space=pltpu.SMEM)
NT = (((1,), (1,)), ((), ()))
TN = (((0,), (0,)), ((), ()))
NN = (((1,), (0,)), ((), ()))


def dot(left, right, dims):
    return lax.dot_general(left, right, dims, preferred_element_type=jnp.float32)


def cols(head):
    return slice(head * HD, (head + 1) * HD)


def place(offsets, me, head, level):
    half = 1 << (level - 1)
    shift = offsets[head, level] & (2 * half - 1)
    return (me & (half - 1)) == (shift >> 1), shift & 1


def block_rows(block):
    return pl.ds(pl.multiple_of(block * BLOCK, BLOCK), BLOCK)


def scale_rows(rows, gain):
    return (rows.astype(jnp.float32) * gain).astype(jnp.bfloat16)


def pack_kernel(offsets_in, k_in, v_in, q_in, d_in, norm_in, *refs):
    outs, (offsets, k, v, q, d, norm, sems) = refs[:8], refs[8:]
    copies = []
    for i, (source, target) in enumerate(
        ((offsets_in, offsets), (k_in, k), (v_in, v), (norm_in, norm), (d_in, d), (q_in, q))
    ):
        copies.append(pltpu.make_async_copy(source, target, sems.at[i]))
        copies[-1].start()
    for copy in copies[:5]:
        copy.wait()
    spots = [(level, head, offsets[head, level] & 1) for level in range(1, LEVELS) for head in range(HEADS)]
    row = lax.broadcasted_iota(jnp.int32, (16, BLOCK), 0)
    for level, head, block in spots:
        at, out = block_rows(block), outs[level - 1]
        out[head, :BLOCK] = k[at, cols(head)]
        out[head, BLOCK:PARTS] = v[at, cols(head)]
        out[head, TAIL:] = d[pl.ds(pl.multiple_of(block * BLOCK + BLOCK - EARLY, EARLY), EARLY), cols(head)]
        whole = jnp.where(block == 0, norm[head : head + 1, :BLOCK], norm[head : head + 1, BLOCK:])
        high = whole.astype(jnp.bfloat16).astype(jnp.float32)
        rest = whole - high
        mid = rest.astype(jnp.bfloat16).astype(jnp.float32)
        low = rest - mid
        parts = jnp.where(row == 0, high, jnp.where(row == 1, mid, jnp.where(row == 2, low, 0.0)))
        out[head, PARTS:TAIL] = parts.astype(jnp.bfloat16)
    for copy in copies[5:]:
        copy.wait()
    for level, head, block in spots:
        at, out = block_rows(block), outs[LEVELS - 1 + level - 1]
        out[head, :BLOCK] = q[at, cols(head)]
        out[head, BLOCK:] = d[pl.ds(pl.multiple_of(block * BLOCK, BLOCK), BLOCK - EARLY), cols(head)]


def block_counts(offsets, head):
    me = lax.axis_index("ctx")
    count = [jnp.float32(1.0), jnp.float32(1.0)]
    for level in range(1, LEVELS):
        active, block = place(offsets, me, head, level)
        for b in range(2):
            count[b] = count[b] + jnp.where(active & (block == b), 1.0, 0.0)
    return count


def both_blocks(b):
    return slice(b * BLOCK, (b + 1) * BLOCK), slice((1 - b) * BLOCK, (2 - b) * BLOCK)


def local_q_kernel(offsets, gain, q, k, v, d, norm, dq, norm_cols, scaled):
    for head in range(HEADS):
        c = cols(head)
        count = block_counts(offsets, head)
        query, key, value, dout = scale_rows(q[:, c], gain[:, c]), k[:, c], v[:, c], d[:, c]
        scaled[:, c] = query
        column = jnp.transpose(jnp.broadcast_to(norm[head : head + 1, :], (BLOCK, 2 * BLOCK)))
        norm_cols[head] = column
        probs = jnp.exp(dot(query, key, NT) * SCALE - jnp.concatenate([column, column], axis=1))
        grads = (probs * dot(dout, value, NT)).astype(jnp.bfloat16)
        for b in range(2):
            own, other = both_blocks(b)
            dq[own, c] = count[b] * dot(grads[own, own], key[own], NN) + dot(grads[own, other], key[other], NN)


def local_kv_kernel(offsets, scaled, k, v, d, norm, dk, dv):
    for head in range(HEADS):
        c = cols(head)
        count = block_counts(offsets, head)
        query, key, value, dout = scaled[:, c], k[:, c], v[:, c], d[:, c]
        probs = jnp.exp(dot(key, query, NT) * SCALE - norm[head : head + 1, :])
        grads = (probs * dot(value, dout, NT)).astype(jnp.bfloat16)
        probs = probs.astype(jnp.bfloat16)
        for b in range(2):
            own, other = both_blocks(b)
            dk[own, c] = count[b] * dot(grads[own, own], query[own], NN) + dot(grads[own, other], query[other], NN)
            dv[own, c] = count[b] * dot(probs[own, own], dout[own], NN) + dot(probs[own, other], dout[other], NN)


def for_each_level(offsets, fn):
    me = lax.axis_index("ctx")
    for level in range(1, LEVELS):
        spots = [place(offsets, me, head, level) for head in range(HEADS)]

        def both(level=level, spots=spots):
            fn(level, spots)

        if level == 1:
            both()
        else:
            pl.when(spots[0][0] | spots[1][0])(both)


def query_kernel(offsets, scaled, q, d, norm_cols, dq_in, r1, r2, r3, r4, p1, p2, p3, p4, dq, partial, *passed):
    received = (r1, r2, r3, r4)
    dq[...] = dq_in[...]

    def one(level, spots):
        got = received[level - 1]
        for head in range(HEADS):
            active, block = spots[head]
            c, at = cols(head), block_rows(block)
            key, value = got[head, :BLOCK], got[head, BLOCK:PARTS]
            probs = jnp.exp(dot(scaled[at, c], key, NT) * SCALE - norm_cols[head, at, :])
            grads = (probs * dot(d[at, c], value, NT)).astype(jnp.bfloat16)
            dq[at, c] += jnp.where(active, dot(grads, key, NN), 0.0)

    for_each_level(offsets, one)
    total = jnp.sum(q[...].astype(jnp.float32) * (dq[...] * SCALE), axis=0, keepdims=True)
    partial[...] = jnp.broadcast_to(total[None], partial.shape)


def key_kernel(offsets, gain, k, v, dq, dk_in, dv_in, f1, f2, f3, f4, r1, r2, r3, r4, grad_q, grad_k, grad_v, dk, dv):
    received, firsts = (r1, r2, r3, r4), (f1, f2, f3, f4)
    dk[...] = dk_in[...]
    dv[...] = dv_in[...]
    grad_q[...] = (dq[...] * SCALE * gain[...]).astype(jnp.bfloat16)

    def one(level, spots):
        got = received[level - 1]
        for head in range(HEADS):
            active, block = spots[head]
            c, at = cols(head), block_rows(block)
            query = scale_rows(got[head, :BLOCK], gain[:, c])
            first = firsts[level - 1]
            dout = jnp.concatenate([got[head, BLOCK:], first[head, TAIL:]], axis=0)
            parts = first[head, PARTS:TAIL].astype(jnp.float32)
            norm = parts[0:1] + parts[1:2] + parts[2:3]
            probs = jnp.exp(dot(k[at, c], query, NT) * SCALE - norm)
            grads = (probs * dot(v[at, c], dout, NT)).astype(jnp.bfloat16)
            dk[at, c] += jnp.where(active, dot(grads, query, NN), 0.0)
            dv[at, c] += jnp.where(active, dot(probs.astype(jnp.bfloat16), dout, NN), 0.0)

    for_each_level(offsets, one)
    grad_k[...] = (dk[...] * SCALE).astype(jnp.bfloat16)
    grad_v[...] = dv[...].astype(jnp.bfloat16)


def call(kernel, name, outs, in_specs, scratch=(), out_specs=None, aliases=None):
    return pl.pallas_call(
        kernel,
        name=name,
        out_shape=outs,
        in_specs=in_specs,
        out_specs=out_specs or [VMEM] * len(outs),
        scratch_shapes=list(scratch),
        input_output_aliases=aliases or {},
        compiler_params=pltpu.CompilerParams(vmem_limit_bytes=32 * 1024 * 1024),
    )


def in_hbm(array):
    return pltpu.with_memory_space_constraint(array, pltpu.HBM)


def swap(payloads):
    count = lax.axis_size("ctx")
    return [lax.ppermute(p, "ctx", [(i, i ^ (1 << n)) for i in range(count)]) for n, p in enumerate(payloads)]


def body(queries, keys, values, grad_out, log_norm, offsets, q_gain):
    q, k, v, d = queries[0], keys[0], values[0], grad_out[0]
    norm = log_norm[0]
    tokens, width = q.shape
    gain = q_gain.reshape(1, width)
    f32 = functools.partial(jax.ShapeDtypeStruct, dtype=jnp.float32)
    bf16 = functools.partial(jax.ShapeDtypeStruct, dtype=jnp.bfloat16)
    many = LEVELS - 1
    raw = pltpu.VMEM((tokens, width), jnp.bfloat16)
    sent = call(
        pack_kernel,
        "pack",
        [bf16((HEADS, FIRST, HD))] * many + [bf16((HEADS, SECOND, HD))] * many,
        [HBM] * 6,
        [
            pltpu.SMEM(offsets.shape, jnp.int32),
            raw,
            raw,
            raw,
            raw,
            pltpu.VMEM(norm.shape, jnp.float32),
            pltpu.SemaphoreType.DMA((6,)),
        ],
    )(*map(in_hbm, (offsets, k, v, q, d, norm)))
    got_kv = swap(sent[:many])
    dq, norm_cols, scaled = call(
        local_q_kernel,
        "local_q",
        [f32((tokens, width)), f32((HEADS, tokens, HD)), bf16((tokens, width))],
        [SMEM] + [VMEM] * 6,
    )(offsets, gain, q, k, v, d, norm)
    axes = ("dp", "ctx")
    everyone = lax.axis_size(axes)
    dq, partial, *later = call(
        query_kernel,
        "remote_q",
        [f32((tokens, width)), f32((everyone, 1, width))] + [bf16((HEADS, SECOND, HD))] * many,
        [SMEM] + [VMEM] * 9 + [ANY] * many,
        out_specs=[VMEM] * 2 + [ANY] * many,
        aliases={10 + i: 2 + i for i in range(many)},
    )(offsets, scaled, q, d, norm_cols, dq, *got_kv, *sent[many:])
    parts = lax.all_to_all(partial, axes, 0, 0, tiled=True)
    dk, dv = call(local_kv_kernel, "local_kv", [f32((tokens, width))] * 2, [SMEM] + [VMEM] * 5)(
        offsets, scaled, k, v, d, norm
    )
    got_qd = swap(later)
    acc = pltpu.VMEM((tokens, width), jnp.float32)
    grad_q, grad_k, grad_v = call(
        key_kernel, "remote_kv", [bf16((tokens, width))] * 3, [SMEM] + [VMEM] * 14, [acc, acc]
    )(offsets, gain, k, v, dq, dk, dv, *got_kv, *got_qd)
    return (grad_q[None], grad_k[None], grad_v[None], jnp.sum(parts, axis=(0, 1)))


def solution(mesh):
    rows = P("dp", "ctx", None)
    in_specs = (rows, rows, rows, rows, P("dp", None, "ctx"), P(), P())
    out_specs = (rows, rows, rows, P())
    return jax.shard_map(body, mesh=mesh, in_specs=in_specs, out_specs=out_specs, check_vma=False)
```

```python
import functools

import jax
import jax.numpy as jnp
from jax import lax
from jax.experimental import pallas as pl
from jax.experimental.pallas import tpu as pltpu
from jax.sharding import PartitionSpec as P

BLOCK = 128
LEVELS = 5
HEADS = 2
HD = 128
SCALE = HD**-0.5
ROW_Q, ROW_D, ROW_N, ROWS = 0, 128, 256, 272

HBM = pl.BlockSpec(memory_space=pltpu.HBM)
ANY = pl.BlockSpec(memory_space=pl.ANY)
VMEM = pl.BlockSpec(memory_space=pltpu.VMEM)
SMEM = pl.BlockSpec(memory_space=pltpu.SMEM)
ORDER = (4, 1, 2, 3)
NT = (((1,), (1,)), ((), ()))
TN = (((0,), (0,)), ((), ()))
NN = (((1,), (0,)), ((), ()))


def dot(left, right, dims):
    return lax.dot_general(left, right, dims, preferred_element_type=jnp.float32)


def cols(head):
    return slice(head * HD, (head + 1) * HD)


def place(offsets, me, head, level):
    half = 1 << (level - 1)
    shift = offsets[head, level] & (2 * half - 1)
    return (me & (half - 1)) == (shift >> 1), shift & 1


def block_rows(block):
    return pl.ds(pl.multiple_of(block * BLOCK, BLOCK), BLOCK)


def scale_rows(rows, gain):
    return (rows.astype(jnp.float32) * gain).astype(jnp.bfloat16)


def pack_kernel(offsets_in, k_in, v_in, q_in, d_in, norm_in, *refs):
    outs, (offsets, k, v, q, d, norm, sems) = refs[:8], refs[8:]
    copies = []
    for i, (source, target) in enumerate(
        ((offsets_in, offsets), (k_in, k), (v_in, v), (q_in, q), (d_in, d), (norm_in, norm))
    ):
        copies.append(pltpu.make_async_copy(source, target, sems.at[i]))
        copies[-1].start()
    for copy in copies[:3]:
        copy.wait()
    spots = [(level, head, offsets[head, level] & 1) for level in range(1, LEVELS) for head in range(HEADS)]
    for level, head, block in spots:
        at, out = block_rows(block), outs[level - 1]
        out[head, :BLOCK] = k[at, cols(head)]
        out[head, BLOCK:] = v[at, cols(head)]
    for copy in copies[3:]:
        copy.wait()
    row = lax.broadcasted_iota(jnp.int32, (16, BLOCK), 0)
    for level, head, block in spots:
        at, out = block_rows(block), outs[LEVELS - 1 + level - 1]
        out[head, ROW_Q : ROW_Q + BLOCK] = q[at, cols(head)]
        out[head, ROW_D : ROW_D + BLOCK] = d[at, cols(head)]
        whole = jnp.where(block == 0, norm[head : head + 1, :BLOCK], norm[head : head + 1, BLOCK:])
        high = whole.astype(jnp.bfloat16).astype(jnp.float32)
        rest = whole - high
        mid = rest.astype(jnp.bfloat16).astype(jnp.float32)
        low = rest - mid
        parts = jnp.where(row == 0, high, jnp.where(row == 1, mid, jnp.where(row == 2, low, 0.0)))
        out[head, ROW_N:ROWS] = parts.astype(jnp.bfloat16)


def block_counts(offsets, head):
    me = lax.axis_index("ctx")
    count = [jnp.float32(1.0), jnp.float32(1.0)]
    for level in range(1, LEVELS):
        active, block = place(offsets, me, head, level)
        for b in range(2):
            count[b] = count[b] + jnp.where(active & (block == b), 1.0, 0.0)
    return count


def both_blocks(b):
    return slice(b * BLOCK, (b + 1) * BLOCK), slice((1 - b) * BLOCK, (2 - b) * BLOCK)


def local_q_kernel(offsets, gain, q, k, v, d, norm, dq, norm_cols, scaled, partial):
    for head in range(HEADS):
        c = cols(head)
        count = block_counts(offsets, head)
        query, key, value, dout = scale_rows(q[:, c], gain[:, c]), k[:, c], v[:, c], d[:, c]
        scaled[:, c] = query
        column = jnp.transpose(jnp.broadcast_to(norm[head : head + 1, :], (BLOCK, 2 * BLOCK)))
        norm_cols[head] = column
        probs = jnp.exp(dot(query, key, NT) * SCALE - jnp.concatenate([column, column], axis=1))
        grads = (probs * dot(dout, value, NT)).astype(jnp.bfloat16)
        for b in range(2):
            own, other = both_blocks(b)
            dq[own, c] = count[b] * dot(grads[own, own], key[own], NN) + dot(grads[own, other], key[other], NN)
        partial[:, c] = jnp.sum(q[:, c].astype(jnp.float32) * dq[:, c], axis=0, keepdims=True)


def local_kv_kernel(offsets, scaled, k, v, d, norm, dk, dv):
    for head in range(HEADS):
        c = cols(head)
        count = block_counts(offsets, head)
        query, key, value, dout = scaled[:, c], k[:, c], v[:, c], d[:, c]
        probs = jnp.exp(dot(key, query, NT) * SCALE - norm[head : head + 1, :])
        grads = (probs * dot(value, dout, NT)).astype(jnp.bfloat16)
        probs = probs.astype(jnp.bfloat16)
        for b in range(2):
            own, other = both_blocks(b)
            dk[own, c] = count[b] * dot(grads[own, own], query[own], NN) + dot(grads[own, other], query[other], NN)
            dv[own, c] = count[b] * dot(probs[own, own], dout[own], NN) + dot(probs[own, other], dout[other], NN)


def for_each_level(offsets, fn):
    me = lax.axis_index("ctx")
    for level in range(1, LEVELS):
        spots = [place(offsets, me, head, level) for head in range(HEADS)]

        def both(level=level, spots=spots):
            fn(level, spots)

        if level == 1:
            both()
        else:
            pl.when(spots[0][0] | spots[1][0])(both)


def query_kernel(offsets, scaled, q, d, norm_cols, partial_in, r1, r2, r3, r4, added, partial, total):
    received = dict(zip(ORDER, (r1, r2, r3, r4)))
    total[...] = partial_in[...]

    def one(level, spots):
        got = received[level]
        for head in range(HEADS):
            active, block = spots[head]
            c, at = cols(head), block_rows(block)
            key, value = got[head, :BLOCK], got[head, BLOCK:]
            probs = jnp.exp(dot(scaled[at, c], key, NT) * SCALE - norm_cols[head, at, :])
            grads = (probs * dot(d[at, c], value, NT)).astype(jnp.bfloat16)
            more = jnp.where(active, dot(grads, key, NN), 0.0)
            added[level - 1, head] = more
            total[:, c] += jnp.sum(q[at, c].astype(jnp.float32) * more, axis=0, keepdims=True)

    for_each_level(offsets, one)
    partial[...] = jnp.broadcast_to((total[...] * SCALE)[None], partial.shape)


def key_kernel(offsets, gain, k, v, dq_in, added, dk_in, dv_in, r1, r2, r3, r4, grad_q, grad_k, grad_v, dq, dk, dv):
    received = dict(zip(ORDER, (r1, r2, r3, r4)))
    dq[...] = dq_in[...]
    dk[...] = dk_in[...]
    dv[...] = dv_in[...]

    def one(level, spots):
        got = received[level]
        for head in range(HEADS):
            active, block = spots[head]
            c, at = cols(head), block_rows(block)
            query = scale_rows(got[head, ROW_Q : ROW_Q + BLOCK], gain[:, c])
            dout = got[head, ROW_D : ROW_D + BLOCK]
            parts = got[head, ROW_N:ROWS].astype(jnp.float32)
            norm = parts[0:1] + parts[1:2] + parts[2:3]
            probs = jnp.exp(dot(k[at, c], query, NT) * SCALE - norm)
            grads = (probs * dot(v[at, c], dout, NT)).astype(jnp.bfloat16)
            dq[at, c] += added[level - 1, head]
            dk[at, c] += jnp.where(active, dot(grads, query, NN), 0.0)
            dv[at, c] += jnp.where(active, dot(probs.astype(jnp.bfloat16), dout, NN), 0.0)

    for_each_level(offsets, one)
    grad_q[...] = (dq[...] * SCALE * gain[...]).astype(jnp.bfloat16)
    grad_k[...] = (dk[...] * SCALE).astype(jnp.bfloat16)
    grad_v[...] = dv[...].astype(jnp.bfloat16)


def call(kernel, name, outs, in_specs, scratch=(), out_specs=None, aliases=None):
    return pl.pallas_call(
        kernel,
        name=name,
        out_shape=outs,
        in_specs=in_specs,
        out_specs=out_specs or [VMEM] * len(outs),
        scratch_shapes=list(scratch),
        input_output_aliases=aliases or {},
        compiler_params=pltpu.CompilerParams(vmem_limit_bytes=32 * 1024 * 1024),
    )


def in_hbm(array):
    return pltpu.with_memory_space_constraint(array, pltpu.HBM)


def swap(payloads, order=ORDER):
    count, got = lax.axis_size("ctx"), {}
    for level in order:
        half = 1 << (level - 1)
        got[level] = lax.ppermute(payloads[level - 1], "ctx", [(i, i ^ half) for i in range(count)])
    return [got[level] for level in order]


def body(queries, keys, values, grad_out, log_norm, offsets, q_gain):
    q, k, v, d = queries[0], keys[0], values[0], grad_out[0]
    norm = log_norm[0]
    tokens, width = q.shape
    gain = q_gain.reshape(1, width)
    f32 = functools.partial(jax.ShapeDtypeStruct, dtype=jnp.float32)
    bf16 = functools.partial(jax.ShapeDtypeStruct, dtype=jnp.bfloat16)
    many = LEVELS - 1
    raw = pltpu.VMEM((tokens, width), jnp.bfloat16)
    sent = call(
        pack_kernel,
        "pack",
        [bf16((HEADS, 2 * BLOCK, HD))] * many + [bf16((HEADS, ROWS, HD))] * many,
        [HBM] * 6,
        [
            pltpu.SMEM(offsets.shape, jnp.int32),
            raw,
            raw,
            raw,
            raw,
            pltpu.VMEM(norm.shape, jnp.float32),
            pltpu.SemaphoreType.DMA((6,)),
        ],
    )(*map(in_hbm, (offsets, k, v, q, d, norm)))
    got_kv, got_qd = swap(sent[:many]), swap(sent[many:])
    dq, norm_cols, scaled, partial = call(
        local_q_kernel,
        "local_q",
        [f32((tokens, width)), f32((HEADS, tokens, HD)), bf16((tokens, width)), f32((1, width))],
        [SMEM] + [VMEM] * 6,
    )(offsets, gain, q, k, v, d, norm)
    axes = ("dp", "ctx")
    everyone = lax.axis_size(axes)
    added, partial = call(
        query_kernel,
        "remote_q",
        [f32((many, HEADS, BLOCK, HD)), f32((everyone, 1, width))],
        [SMEM] + [VMEM] * 9,
        [pltpu.VMEM((1, width), jnp.float32)],
    )(offsets, scaled, q, d, norm_cols, partial, *got_kv)
    parts = lax.all_to_all(partial, axes, 0, 0, tiled=True)
    dk, dv = call(local_kv_kernel, "local_kv", [f32((tokens, width))] * 2, [SMEM] + [VMEM] * 5)(
        offsets, scaled, k, v, d, norm
    )
    acc = pltpu.VMEM((tokens, width), jnp.float32)
    grad_q, grad_k, grad_v = call(
        key_kernel, "remote_kv", [bf16((tokens, width))] * 3, [SMEM] + [VMEM] * 11, [acc] * 3
    )(offsets, gain, k, v, dq, added, dk, dv, *got_qd)
    return (grad_q[None], grad_k[None], grad_v[None], jnp.sum(parts, axis=(0, 1)))


def solution(mesh):
    rows = P("dp", "ctx", None)
    in_specs = (rows, rows, rows, rows, P("dp", None, "ctx"), P(), P())
    out_specs = (rows, rows, rows, P())
    return jax.shard_map(body, mesh=mesh, in_specs=in_specs, out_specs=out_specs, check_vma=False)
```

```python
import functools

import jax
import jax.numpy as jnp
from jax import lax
from jax.experimental import pallas as pl
from jax.experimental.pallas import tpu as pltpu
from jax.sharding import PartitionSpec as P

BLOCK = 128
LEVELS = 5
HEADS = 2
HD = 128
SCALE = HD**-0.5
LATE, EARLY, PARTS = (4,), 16, 16

HBM = pl.BlockSpec(memory_space=pltpu.HBM)
ANY = pl.BlockSpec(memory_space=pl.ANY)
VMEM = pl.BlockSpec(memory_space=pltpu.VMEM)
SMEM = pl.BlockSpec(memory_space=pltpu.SMEM)
ORDER = (4, 1, 2, 3)
SOON = tuple(level for level in ORDER if level not in LATE)
NT = (((1,), (1,)), ((), ()))
TN = (((0,), (0,)), ((), ()))
NN = (((1,), (0,)), ((), ()))


def dot(left, right, dims):
    return lax.dot_general(left, right, dims, preferred_element_type=jnp.float32)


def cols(head):
    return slice(head * HD, (head + 1) * HD)


def place(offsets, me, head, level):
    half = 1 << (level - 1)
    shift = offsets[head, level] & (2 * half - 1)
    return (me & (half - 1)) == (shift >> 1), shift & 1


def block_rows(block):
    return pl.ds(pl.multiple_of(block * BLOCK, BLOCK), BLOCK)


def scale_rows(rows, gain):
    return (rows.astype(jnp.float32) * gain).astype(jnp.bfloat16)


def pack_kernel(offsets_in, k_in, v_in, q_in, d_in, norm_in, gain_in, *refs):
    outs, (norm, gain, table), (offsets, k, v, q, d, sems) = refs[:8], refs[8:11], refs[11:]
    copies = []
    moves = ((offsets_in, offsets), (k_in, k), (v_in, v), (q_in, q), (d_in, d))
    for i, (source, target) in enumerate(moves + ((norm_in, norm), (gain_in, gain), (offsets_in, table))):
        copies.append(pltpu.make_async_copy(source, target, sems.at[i]))
        copies[-1].start()
    for copy in copies:
        copy.wait()
    row = lax.broadcasted_iota(jnp.int32, (PARTS, BLOCK), 0)
    for level in range(1, LEVELS):
        first, second = outs[level - 1], outs[LEVELS - 1 + level - 1]
        for head in range(HEADS):
            block, c = offsets[head, level] & 1, cols(head)
            at = block_rows(block)
            first[head, :BLOCK] = k[at, c]
            first[head, BLOCK : 2 * BLOCK] = v[at, c]
            second[head, :BLOCK] = q[at, c]
            whole = jnp.where(block == 0, norm[head : head + 1, :BLOCK], norm[head : head + 1, BLOCK:])
            high = whole.astype(jnp.bfloat16).astype(jnp.float32)
            rest = whole - high
            mid = rest.astype(jnp.bfloat16).astype(jnp.float32)
            low = rest - mid
            parts = jnp.where(row == 0, high, jnp.where(row == 1, mid, jnp.where(row == 2, low, 0.0)))
            parts = parts.astype(jnp.bfloat16)
            if level in LATE:
                start = pl.multiple_of(block * BLOCK, BLOCK)
                first[head, 2 * BLOCK : 2 * BLOCK + PARTS] = parts
                first[head, 2 * BLOCK + PARTS :] = d[pl.ds(start + BLOCK - EARLY, EARLY), c]
                second[head, BLOCK:] = d[pl.ds(start, BLOCK - EARLY), c]
            else:
                second[head, BLOCK : 2 * BLOCK] = d[at, c]
                second[head, 2 * BLOCK :] = parts


def block_counts(offsets, head):
    me = lax.axis_index("ctx")
    count = [jnp.float32(1.0), jnp.float32(1.0)]
    for level in range(1, LEVELS):
        active, block = place(offsets, me, head, level)
        for b in range(2):
            count[b] = count[b] + jnp.where(active & (block == b), 1.0, 0.0)
    return count


def both_blocks(b):
    return slice(b * BLOCK, (b + 1) * BLOCK), slice((1 - b) * BLOCK, (2 - b) * BLOCK)


def local_q_kernel(offsets, gain, q, k, v, d, norm, *refs):
    dq, norm_cols, scaled, partial = refs[LEVELS - 1 - len(LATE) :][:4]
    for head in range(HEADS):
        c = cols(head)
        count = block_counts(offsets, head)
        query, key, value, dout = scale_rows(q[:, c], gain[:, c]), k[:, c], v[:, c], d[:, c]
        scaled[:, c] = query
        column = jnp.transpose(jnp.broadcast_to(norm[head : head + 1, :], (BLOCK, 2 * BLOCK)))
        norm_cols[head] = column
        probs = jnp.exp(dot(query, key, NT) * SCALE - jnp.concatenate([column, column], axis=1))
        grads = (probs * dot(dout, value, NT)).astype(jnp.bfloat16)
        for b in range(2):
            own, other = both_blocks(b)
            dq[own, c] = count[b] * dot(grads[own, own], key[own], NN) + dot(grads[own, other], key[other], NN)
        partial[:, c] = jnp.sum(q[:, c].astype(jnp.float32) * dq[:, c], axis=0, keepdims=True)


def for_each_level(offsets, levels, fn):
    me = lax.axis_index("ctx")
    for level in levels:
        spots = [place(offsets, me, head, level) for head in range(HEADS)]

        def both(level=level, spots=spots):
            fn(level, spots)

        if level == 1:
            both()
        else:
            pl.when(spots[0][0] | spots[1][0])(both)


def query_kernel(offsets, scaled, q, d, norm_cols, partial_in, r1, r2, r3, r4, *refs):
    added, partial, total = refs[len(LATE)], refs[len(LATE) + 1], refs[-1]
    received = dict(zip(ORDER, (r1, r2, r3, r4)))
    total[...] = partial_in[...]

    def one(level, spots):
        got = received[level]
        for head in range(HEADS):
            active, block = spots[head]
            c, at = cols(head), block_rows(block)
            key, value = got[head, :BLOCK], got[head, BLOCK : 2 * BLOCK]
            probs = jnp.exp(dot(scaled[at, c], key, NT) * SCALE - norm_cols[head, at, :])
            grads = (probs * dot(d[at, c], value, NT)).astype(jnp.bfloat16)
            more = jnp.where(active, dot(grads, key, NN), 0.0)
            added[level - 1, head] = more
            total[:, c] += jnp.sum(q[at, c].astype(jnp.float32) * more, axis=0, keepdims=True)

    for_each_level(offsets, range(1, LEVELS), one)
    partial[...] = jnp.broadcast_to((total[...] * SCALE)[None], partial.shape)


def add_keys(level, spots, got, first, gain, k, v, dk, dv):
    for head in range(HEADS):
        active, block = spots[head]
        c, at = cols(head), block_rows(block)
        query = scale_rows(got[head, :BLOCK], gain[:, c])
        if level in LATE:
            parts = first[head, 2 * BLOCK : 2 * BLOCK + PARTS]
            dout = jnp.concatenate([got[head, BLOCK:], first[head, 2 * BLOCK + PARTS :]], axis=0)
        else:
            parts, dout = got[head, 2 * BLOCK :], got[head, BLOCK : 2 * BLOCK]
        parts = parts.astype(jnp.float32)
        norm = parts[0:1] + parts[1:2] + parts[2:3]
        probs = jnp.exp(dot(k[at, c], query, NT) * SCALE - norm)
        grads = (probs * dot(v[at, c], dout, NT)).astype(jnp.bfloat16)
        dk[at, c] += jnp.where(active, dot(grads, query, NN), 0.0)
        dv[at, c] += jnp.where(active, dot(probs.astype(jnp.bfloat16), dout, NN), 0.0)


def most_kernel(offsets, gain, scaled, k, v, d, norm, dq_in, added, r1, r2, r3, grad_q, dk, dv, dq):
    received = dict(zip(SOON, (r1, r2, r3)))
    for head in range(HEADS):
        c = cols(head)
        count = block_counts(offsets, head)
        query, key, value, dout = scaled[:, c], k[:, c], v[:, c], d[:, c]
        probs = jnp.exp(dot(key, query, NT) * SCALE - norm[head : head + 1, :])
        grads = (probs * dot(value, dout, NT)).astype(jnp.bfloat16)
        probs = probs.astype(jnp.bfloat16)
        for b in range(2):
            own, other = both_blocks(b)
            dk[own, c] = count[b] * dot(grads[own, own], query[own], NN) + dot(grads[own, other], query[other], NN)
            dv[own, c] = count[b] * dot(probs[own, own], dout[own], NN) + dot(probs[own, other], dout[other], NN)
    dq[...] = dq_in[...]

    def add_queries(level, spots):
        for head in range(HEADS):
            dq[block_rows(spots[head][1]), cols(head)] += added[level - 1, head]

    for_each_level(offsets, range(1, LEVELS), add_queries)
    grad_q[...] = (dq[...] * SCALE * gain[...]).astype(jnp.bfloat16)
    for_each_level(
        offsets, SOON, lambda level, spots: add_keys(level, spots, received[level], None, gain, k, v, dk, dv)
    )


def last_kernel(offsets, gain, k, v, dk_in, dv_in, got, first, grad_k, grad_v, dk, dv):
    dk[...] = dk_in[...]
    dv[...] = dv_in[...]
    for_each_level(offsets, LATE, lambda level, spots: add_keys(level, spots, got, first, gain, k, v, dk, dv))
    grad_k[...] = (dk[...] * SCALE).astype(jnp.bfloat16)
    grad_v[...] = dv[...].astype(jnp.bfloat16)


def call(kernel, name, outs, in_specs, scratch=(), out_specs=None, aliases=None):
    return pl.pallas_call(
        kernel,
        name=name,
        out_shape=outs,
        in_specs=in_specs,
        out_specs=out_specs or [VMEM] * len(outs),
        scratch_shapes=list(scratch),
        input_output_aliases=aliases or {},
        compiler_params=pltpu.CompilerParams(vmem_limit_bytes=32 * 1024 * 1024),
    )


def in_hbm(array):
    return pltpu.with_memory_space_constraint(array, pltpu.HBM)


def swap(payloads):
    count, got = lax.axis_size("ctx"), {}
    for level, payload in payloads.items():
        half = 1 << (level - 1)
        got[level] = lax.ppermute(payload, "ctx", [(i, i ^ half) for i in range(count)])
    return got


def body(queries, keys, values, grad_out, log_norm, offsets, q_gain):
    q, k, v, d = queries[0], keys[0], values[0], grad_out[0]
    norm = log_norm[0]
    tokens, width = q.shape
    gain = q_gain.reshape(1, width)
    f32 = functools.partial(jax.ShapeDtypeStruct, dtype=jnp.float32)
    bf16 = functools.partial(jax.ShapeDtypeStruct, dtype=jnp.bfloat16)
    many = LEVELS - 1
    raw = pltpu.VMEM((tokens, width), jnp.bfloat16)
    *sent, norm, gain, table = call(
        pack_kernel,
        "pack",
        [bf16((HEADS, 2 * BLOCK + (PARTS + EARLY) * (level in LATE), HD)) for level in range(1, LEVELS)]
        + [bf16((HEADS, 2 * BLOCK + (-EARLY if level in LATE else PARTS), HD)) for level in range(1, LEVELS)]
        + [f32(norm.shape), f32(gain.shape), jax.ShapeDtypeStruct(offsets.shape, jnp.int32)],
        [HBM] * 7,
        [pltpu.SMEM(offsets.shape, jnp.int32), raw, raw, raw, raw, pltpu.SemaphoreType.DMA((8,))],
    )(*map(in_hbm, (offsets, k, v, q, d, norm, gain)))
    offsets = table
    second = dict(zip(range(1, LEVELS), sent[many:]))
    got_kv = swap({level: sent[level - 1] for level in ORDER})
    early = {level: second[level] for level in ORDER if level not in LATE}
    dq, norm_cols, scaled, partial, *passed = call(
        local_q_kernel,
        "local_q",
        [f32((tokens, width)), f32((HEADS, tokens, HD)), bf16((tokens, width)), f32((1, width))]
        + [bf16(p.shape) for p in early.values()],
        [SMEM] + [VMEM] * 6 + [ANY] * len(early),
        out_specs=[VMEM] * 4 + [ANY] * len(early),
        aliases={7 + i: 4 + i for i in range(len(early))},
    )(offsets, gain, q, k, v, d, norm, *early.values())
    got_qd = swap(dict(zip(early, passed)))
    axes = ("dp", "ctx")
    everyone = lax.axis_size(axes)
    late = [second[level] for level in LATE]
    added, partial, *late = call(
        query_kernel,
        "remote_q",
        [f32((many, HEADS, BLOCK, HD)), f32((everyone, 1, width))] + [bf16(p.shape) for p in late],
        [SMEM] + [VMEM] * 9 + [ANY] * len(late),
        [pltpu.VMEM((1, width), jnp.float32)],
        [VMEM] * 2 + [ANY] * len(late),
        {10 + i: 2 + i for i in range(len(late))},
    )(offsets, scaled, q, d, norm_cols, partial, *(got_kv[level] for level in ORDER), *late)
    got_qd.update(swap(dict(zip(LATE, late))))
    parts = lax.all_to_all(partial, axes, 0, 0, tiled=True)
    acc = pltpu.VMEM((tokens, width), jnp.float32)
    grad_q, dk, dv = call(
        most_kernel,
        "most_kv",
        [bf16((tokens, width)), f32((tokens, width)), f32((tokens, width))],
        [SMEM] + [VMEM] * 11,
        [acc],
    )(offsets, gain, scaled, k, v, d, norm, dq, added, *(got_qd[level] for level in SOON))
    grad_k, grad_v = call(
        last_kernel, "last_kv", [bf16((tokens, width))] * 2, [SMEM] + [VMEM] * 7, [acc, acc]
    )(offsets, gain, k, v, dk, dv, got_qd[LATE[0]], got_kv[LATE[0]])
    return (grad_q[None], grad_k[None], grad_v[None], jnp.sum(parts, axis=(0, 1)))


def solution(mesh):
    rows = P("dp", "ctx", None)
    in_specs = (rows, rows, rows, rows, P("dp", None, "ctx"), P(), P())
    out_specs = (rows, rows, rows, P())
    return jax.shard_map(body, mesh=mesh, in_specs=in_specs, out_specs=out_specs, check_vma=False)
```

```python
import functools

import jax
import jax.numpy as jnp
from jax import lax
from jax.experimental import pallas as pl
from jax.experimental.pallas import tpu as pltpu
from jax.sharding import PartitionSpec as P

BLOCK = 128
LEVELS = 5
HEADS = 2
HD = 128
SCALE = HD**-0.5
LATE, EARLY, PARTS = (4,), 16, 16

HBM = pl.BlockSpec(memory_space=pltpu.HBM)
ANY = pl.BlockSpec(memory_space=pl.ANY)
VMEM = pl.BlockSpec(memory_space=pltpu.VMEM)
SMEM = pl.BlockSpec(memory_space=pltpu.SMEM)
ORDER = (4,1,2,3)
SOON = (3,2,1,)
NT = (((1,), (1,)), ((), ()))
TN = (((0,), (0,)), ((), ()))
NN = (((1,), (0,)), ((), ()))


def dot(left, right, dims):
    return lax.dot_general(left, right, dims, preferred_element_type=jnp.float32)


def cols(head):
    return slice(head * HD, (head + 1) * HD)


def place(offsets, me, head, level):
    half = 1 << (level - 1)
    shift = offsets[head, level] & (2 * half - 1)
    return (me & (half - 1)) == (shift >> 1), shift & 1


def block_rows(block):
    return pl.ds(pl.multiple_of(block * BLOCK, BLOCK), BLOCK)


def scale_rows(rows, gain):
    return (rows.astype(jnp.float32) * gain).astype(jnp.bfloat16)


def pack_kernel(offsets_in, k_in, v_in, q_in, d_in, norm_in, gain_in, *refs):
    outs, (norm, gain, table), (offsets, k, v, q, d, sems) = refs[:8], refs[8:11], refs[11:]
    copies = []
    moves = ((offsets_in, offsets), (k_in, k), (v_in, v), (q_in, q), (d_in, d))
    for i, (source, target) in enumerate(moves + ((norm_in, norm), (gain_in, gain), (offsets_in, table))):
        copies.append(pltpu.make_async_copy(source, target, sems.at[i]))
        copies[-1].start()
    for copy in copies:
        copy.wait()
    row = lax.broadcasted_iota(jnp.int32, (PARTS, BLOCK), 0)
    for level in range(1, LEVELS):
        first, second = outs[level - 1], outs[LEVELS - 1 + level - 1]
        for head in range(HEADS):
            block, c = offsets[head, level] & 1, cols(head)
            at = block_rows(block)
            first[head, :BLOCK] = k[at, c]
            first[head, BLOCK : 2 * BLOCK] = v[at, c]
            second[head, :BLOCK] = q[at, c]
            whole = jnp.where(block == 0, norm[head : head + 1, :BLOCK], norm[head : head + 1, BLOCK:])
            high = whole.astype(jnp.bfloat16).astype(jnp.float32)
            rest = whole - high
            mid = rest.astype(jnp.bfloat16).astype(jnp.float32)
            low = rest - mid
            parts = jnp.where(row == 0, high, jnp.where(row == 1, mid, jnp.where(row == 2, low, 0.0)))
            parts = parts.astype(jnp.bfloat16)
            if level in LATE:
                start = pl.multiple_of(block * BLOCK, BLOCK)
                first[head, 2 * BLOCK : 2 * BLOCK + PARTS] = parts
                first[head, 2 * BLOCK + PARTS :] = d[pl.ds(start + BLOCK - EARLY, EARLY), c]
                second[head, BLOCK:] = d[pl.ds(start, BLOCK - EARLY), c]
            else:
                second[head, BLOCK : 2 * BLOCK] = d[at, c]
                second[head, 2 * BLOCK :] = parts


def block_counts(offsets, head):
    me = lax.axis_index("ctx")
    count = [jnp.float32(1.0), jnp.float32(1.0)]
    for level in range(1, LEVELS):
        active, block = place(offsets, me, head, level)
        for b in range(2):
            count[b] = count[b] + jnp.where(active & (block == b), 1.0, 0.0)
    return count


def both_blocks(b):
    return slice(b * BLOCK, (b + 1) * BLOCK), slice((1 - b) * BLOCK, (2 - b) * BLOCK)


def local_q_kernel(offsets, gain, q, k, v, d, norm, *refs):
    dq, norm_cols, scaled, partial = refs[LEVELS - 1 - len(LATE) :][:4]
    for head in range(HEADS):
        c = cols(head)
        count = block_counts(offsets, head)
        query, key, value, dout = scale_rows(q[:, c], gain[:, c]), k[:, c], v[:, c], d[:, c]
        scaled[:, c] = query
        column = jnp.transpose(jnp.broadcast_to(norm[head : head + 1, :], (BLOCK, 2 * BLOCK)))
        norm_cols[head] = column
        probs = jnp.exp(dot(query, key, NT) * SCALE - jnp.concatenate([column, column], axis=1))
        grads = (probs * dot(dout, value, NT)).astype(jnp.bfloat16)
        for b in range(2):
            own, other = both_blocks(b)
            dq[own, c] = count[b] * dot(grads[own, own], key[own], NN) + dot(grads[own, other], key[other], NN)
        partial[:, c] = jnp.sum(q[:, c].astype(jnp.float32) * dq[:, c], axis=0, keepdims=True)


def for_each_level(offsets, levels, fn):
    me = lax.axis_index("ctx")
    for level in levels:
        spots = [place(offsets, me, head, level) for head in range(HEADS)]

        def both(level=level, spots=spots):
            fn(level, spots)

        if level == 1:
            both()
        else:
            pl.when(spots[0][0] | spots[1][0])(both)


def query_kernel(offsets, scaled, q, d, norm_cols, partial_in, r1, r2, r3, r4, *refs):
    added, partial, total = refs[len(LATE)], refs[len(LATE) + 1], refs[-1]
    received = dict(zip(ORDER, (r1, r2, r3, r4)))
    total[...] = partial_in[...]

    def one(level, spots):
        got = received[level]
        for head in range(HEADS):
            active, block = spots[head]
            c, at = cols(head), block_rows(block)
            key, value = got[head, :BLOCK], got[head, BLOCK : 2 * BLOCK]
            probs = jnp.exp(dot(scaled[at, c], key, NT) * SCALE - norm_cols[head, at, :])
            grads = (probs * dot(d[at, c], value, NT)).astype(jnp.bfloat16)
            more = jnp.where(active, dot(grads, key, NN), 0.0)
            added[level - 1, head] = more
            total[:, c] += jnp.sum(q[at, c].astype(jnp.float32) * more, axis=0, keepdims=True)

    for_each_level(offsets, range(1, LEVELS), one)
    partial[...] = jnp.broadcast_to((total[...] * SCALE)[None], partial.shape)


def add_keys(level, spots, got, first, gain, k, v, dk, dv):
    for head in range(HEADS):
        active, block = spots[head]
        c, at = cols(head), block_rows(block)
        query = scale_rows(got[head, :BLOCK], gain[:, c])
        if level in LATE:
            parts = first[head, 2 * BLOCK : 2 * BLOCK + PARTS]
            dout = jnp.concatenate([got[head, BLOCK:], first[head, 2 * BLOCK + PARTS :]], axis=0)
        else:
            parts, dout = got[head, 2 * BLOCK :], got[head, BLOCK : 2 * BLOCK]
        parts = parts.astype(jnp.float32)
        norm = parts[0:1] + parts[1:2] + parts[2:3]
        probs = jnp.exp(dot(k[at, c], query, NT) * SCALE - norm)
        grads = (probs * dot(v[at, c], dout, NT)).astype(jnp.bfloat16)
        dk[at, c] += jnp.where(active, dot(grads, query, NN), 0.0)
        dv[at, c] += jnp.where(active, dot(probs.astype(jnp.bfloat16), dout, NN), 0.0)


def most_kernel(offsets, gain, scaled, k, v, d, norm, dq_in, added, *refs):
    received, (grad_q, dk, dv, dq) = dict(zip(SOON, refs)), refs[len(SOON) :]
    for head in range(HEADS):
        c = cols(head)
        count = block_counts(offsets, head)
        query, key, value, dout = scaled[:, c], k[:, c], v[:, c], d[:, c]
        probs = jnp.exp(dot(key, query, NT) * SCALE - norm[head : head + 1, :])
        grads = (probs * dot(value, dout, NT)).astype(jnp.bfloat16)
        probs = probs.astype(jnp.bfloat16)
        for b in range(2):
            own, other = both_blocks(b)
            dk[own, c] = count[b] * dot(grads[own, own], query[own], NN) + dot(grads[own, other], query[other], NN)
            dv[own, c] = count[b] * dot(probs[own, own], dout[own], NN) + dot(probs[own, other], dout[other], NN)
    dq[...] = dq_in[...]

    def add_queries(level, spots):
        for head in range(HEADS):
            dq[block_rows(spots[head][1]), cols(head)] += added[level - 1, head]

    for_each_level(offsets, range(1, LEVELS), add_queries)
    grad_q[...] = (dq[...] * SCALE * gain[...]).astype(jnp.bfloat16)
    for_each_level(
        offsets, SOON, lambda level, spots: add_keys(level, spots, received[level], None, gain, k, v, dk, dv)
    )


def last_kernel(offsets, gain, k, v, dk_in, dv_in, *refs):
    got, first = dict(zip(LATE, refs)), dict(zip(LATE, refs[len(LATE) :]))
    grad_k, grad_v, dk, dv = refs[2 * len(LATE) :]
    dk[...] = dk_in[...]
    dv[...] = dv_in[...]
    for_each_level(
        offsets, LATE, lambda level, spots: add_keys(level, spots, got[level], first[level], gain, k, v, dk, dv)
    )
    grad_k[...] = (dk[...] * SCALE).astype(jnp.bfloat16)
    grad_v[...] = dv[...].astype(jnp.bfloat16)


def call(kernel, name, outs, in_specs, scratch=(), out_specs=None, aliases=None):
    return pl.pallas_call(
        kernel,
        name=name,
        out_shape=outs,
        in_specs=in_specs,
        out_specs=out_specs or [VMEM] * len(outs),
        scratch_shapes=list(scratch),
        input_output_aliases=aliases or {},
        compiler_params=pltpu.CompilerParams(vmem_limit_bytes=32 * 1024 * 1024),
    )


def in_hbm(array):
    return pltpu.with_memory_space_constraint(array, pltpu.HBM)


def swap(payloads):
    count, got = lax.axis_size("ctx"), {}
    for level, payload in payloads.items():
        half = 1 << (level - 1)
        got[level] = lax.ppermute(payload, "ctx", [(i, i ^ half) for i in range(count)])
    return got


def body(queries, keys, values, grad_out, log_norm, offsets, q_gain):
    q, k, v, d = queries[0], keys[0], values[0], grad_out[0]
    norm = log_norm[0]
    tokens, width = q.shape
    gain = q_gain.reshape(1, width)
    f32 = functools.partial(jax.ShapeDtypeStruct, dtype=jnp.float32)
    bf16 = functools.partial(jax.ShapeDtypeStruct, dtype=jnp.bfloat16)
    many = LEVELS - 1
    raw = pltpu.VMEM((tokens, width), jnp.bfloat16)
    *sent, norm, gain, table = call(
        pack_kernel,
        "pack",
        [bf16((HEADS, 2 * BLOCK + (PARTS + EARLY) * (level in LATE), HD)) for level in range(1, LEVELS)]
        + [bf16((HEADS, 2 * BLOCK + (-EARLY if level in LATE else PARTS), HD)) for level in range(1, LEVELS)]
        + [f32(norm.shape), f32(gain.shape), jax.ShapeDtypeStruct(offsets.shape, jnp.int32)],
        [HBM] * 7,
        [pltpu.SMEM(offsets.shape, jnp.int32), raw, raw, raw, raw, pltpu.SemaphoreType.DMA((8,))],
    )(*map(in_hbm, (offsets, k, v, q, d, norm, gain)))
    offsets = table
    second = dict(zip(range(1, LEVELS), sent[many:]))
    got_kv = swap({level: sent[level - 1] for level in ORDER})
    early = {level: second[level] for level in SOON}
    dq, norm_cols, scaled, partial, *passed = call(
        local_q_kernel,
        "local_q",
        [f32((tokens, width)), f32((HEADS, tokens, HD)), bf16((tokens, width)), f32((1, width))]
        + [bf16(p.shape) for p in early.values()],
        [SMEM] + [VMEM] * 6 + [ANY] * len(early),
        out_specs=[VMEM] * 4 + [ANY] * len(early),
        aliases={7 + i: 4 + i for i in range(len(early))},
    )(offsets, gain, q, k, v, d, norm, *early.values())
    got_qd = swap(dict(zip(early, passed)))
    axes = ("dp", "ctx")
    everyone = lax.axis_size(axes)
    late = [second[level] for level in LATE]
    added, partial, *late = call(
        query_kernel,
        "remote_q",
        [f32((many, HEADS, BLOCK, HD)), f32((everyone, 1, width))] + [bf16(p.shape) for p in late],
        [SMEM] + [VMEM] * 9 + [ANY] * len(late),
        [pltpu.VMEM((1, width), jnp.float32)],
        [VMEM] * 2 + [ANY] * len(late),
        {10 + i: 2 + i for i in range(len(late))},
    )(offsets, scaled, q, d, norm_cols, partial, *(got_kv[level] for level in ORDER), *late)
    got_qd.update(swap(dict(zip(LATE, late))))
    parts = lax.all_to_all(partial, axes, 0, 0, tiled=True)
    acc = pltpu.VMEM((tokens, width), jnp.float32)
    grad_q, dk, dv = call(
        most_kernel,
        "most_kv",
        [bf16((tokens, width)), f32((tokens, width)), f32((tokens, width))],
        [SMEM] + [VMEM] * (8 + len(SOON)),
        [acc],
    )(offsets, gain, scaled, k, v, d, norm, dq, added, *(got_qd[level] for level in SOON))
    grad_k, grad_v = call(
        last_kernel, "last_kv", [bf16((tokens, width))] * 2, [SMEM] + [VMEM] * (5 + 2 * len(LATE)), [acc, acc]
    )(offsets, gain, k, v, dk, dv, *(got_qd[level] for level in LATE), *(got_kv[level] for level in LATE))
    return (grad_q[None], grad_k[None], grad_v[None], jnp.sum(parts, axis=(0, 1)))


def solution(mesh):
    rows = P("dp", "ctx", None)
    in_specs = (rows, rows, rows, rows, P("dp", None, "ctx"), P(), P())
    out_specs = (rows, rows, rows, P())
    return jax.shard_map(body, mesh=mesh, in_specs=in_specs, out_specs=out_specs, check_vma=False)
```

```python
import functools

import jax
import jax.numpy as jnp
from jax import lax
from jax.experimental import pallas as pl
from jax.experimental.pallas import tpu as pltpu
from jax.sharding import PartitionSpec as P

BLOCK = 128
LEVELS = 5
HEADS = 2
HD = 128
SCALE = HD**-0.5
LATE, EARLY, PARTS = (4,), 16, 16

HBM = pl.BlockSpec(memory_space=pltpu.HBM)
ANY = pl.BlockSpec(memory_space=pl.ANY)
VMEM = pl.BlockSpec(memory_space=pltpu.VMEM)
SMEM = pl.BlockSpec(memory_space=pltpu.SMEM)
ORDER = (4,1,2,3)
SOON = (3,2,1,)
NT = (((1,), (1,)), ((), ()))
TN = (((0,), (0,)), ((), ()))
NN = (((1,), (0,)), ((), ()))


def dot(left, right, dims):
    return lax.dot_general(left, right, dims, preferred_element_type=jnp.float32)


def cols(head):
    return slice(head * HD, (head + 1) * HD)


def place(offsets, me, head, level):
    half = 1 << (level - 1)
    shift = offsets[head, level] & (2 * half - 1)
    return (me & (half - 1)) == (shift >> 1), shift & 1


def block_rows(block):
    return pl.ds(pl.multiple_of(block * BLOCK, BLOCK), BLOCK)


def scale_rows(rows, gain):
    return (rows.astype(jnp.float32) * gain).astype(jnp.bfloat16)


def pack_kernel(offsets_in, k_in, v_in, q_in, d_in, norm_in, gain_in, *refs):
    outs, (norm, gain, table), (offsets, k, v, q, d, sems) = refs[:8], refs[8:11], refs[11:]
    copies = []
    moves = ((offsets_in, offsets), (k_in, k), (v_in, v), (q_in, q), (d_in, d))
    for i, (source, target) in enumerate(moves + ((norm_in, norm), (gain_in, gain), (offsets_in, table))):
        copies.append(pltpu.make_async_copy(source, target, sems.at[i]))
        copies[-1].start()
    for copy in copies:
        copy.wait()
    row = lax.broadcasted_iota(jnp.int32, (PARTS, BLOCK), 0)
    for level in range(1, LEVELS):
        first, second = outs[level - 1], outs[LEVELS - 1 + level - 1]
        for head in range(HEADS):
            block, c = offsets[head, level] & 1, cols(head)
            at = block_rows(block)
            first[head, :BLOCK] = k[at, c]
            first[head, BLOCK : 2 * BLOCK] = v[at, c]
            second[head, :BLOCK] = q[at, c]
            whole = jnp.where(block == 0, norm[head : head + 1, :BLOCK], norm[head : head + 1, BLOCK:])
            high = whole.astype(jnp.bfloat16).astype(jnp.float32)
            rest = whole - high
            mid = rest.astype(jnp.bfloat16).astype(jnp.float32)
            low = rest - mid
            parts = jnp.where(row == 0, high, jnp.where(row == 1, mid, jnp.where(row == 2, low, 0.0)))
            parts = parts.astype(jnp.bfloat16)
            if level in LATE:
                start = pl.multiple_of(block * BLOCK, BLOCK)
                first[head, 2 * BLOCK : 2 * BLOCK + PARTS] = parts
                first[head, 2 * BLOCK + PARTS :] = d[pl.ds(start + BLOCK - EARLY, EARLY), c]
                second[head, BLOCK:] = d[pl.ds(start, BLOCK - EARLY), c]
            else:
                second[head, BLOCK : 2 * BLOCK] = d[at, c]
                second[head, 2 * BLOCK :] = parts


def block_counts(offsets, head):
    me = lax.axis_index("ctx")
    count = [jnp.float32(1.0), jnp.float32(1.0)]
    for level in range(1, LEVELS):
        active, block = place(offsets, me, head, level)
        for b in range(2):
            count[b] = count[b] + jnp.where(active & (block == b), 1.0, 0.0)
    return count


def both_blocks(b):
    return slice(b * BLOCK, (b + 1) * BLOCK), slice((1 - b) * BLOCK, (2 - b) * BLOCK)


def local_q_kernel(offsets, gain, q, k, v, d, norm, *refs):
    dq, norm_cols, scaled, partial = refs[LEVELS - 1 - len(LATE) :][:4]
    for head in range(HEADS):
        c = cols(head)
        count = block_counts(offsets, head)
        query, key, value, dout = scale_rows(q[:, c], gain[:, c]), k[:, c], v[:, c], d[:, c]
        scaled[:, c] = query
        column = jnp.transpose(jnp.broadcast_to(norm[head : head + 1, :], (BLOCK, 2 * BLOCK)))
        norm_cols[head] = column
        probs = jnp.exp(dot(query, key, NT) * SCALE - jnp.concatenate([column, column], axis=1))
        grads = (probs * dot(dout, value, NT)).astype(jnp.bfloat16)
        for b in range(2):
            own, other = both_blocks(b)
            dq[own, c] = count[b] * dot(grads[own, own], key[own], NN) + dot(grads[own, other], key[other], NN)
        partial[:, c] = jnp.sum(q[:, c].astype(jnp.float32) * dq[:, c], axis=0, keepdims=True)


def for_each_level(offsets, levels, fn):
    me = lax.axis_index("ctx")
    for level in levels:
        spots = [place(offsets, me, head, level) for head in range(HEADS)]

        def both(level=level, spots=spots):
            fn(level, spots)

        if level == 1:
            both()
        else:
            pl.when(spots[0][0] | spots[1][0])(both)


def query_kernel(offsets, scaled, q, d, norm_cols, partial_in, r1, r2, r3, r4, *refs):
    added, partial, total = refs[len(LATE)], refs[len(LATE) + 1], refs[-1]
    received = dict(zip(ORDER, (r1, r2, r3, r4)))
    total[...] = partial_in[...]

    me = lax.axis_index("ctx")
    spots = {level: [place(offsets, me, head, level) for head in range(HEADS)] for level in range(1, LEVELS)}

    def any_active(level):
        return spots[level][0][0] | spots[level][1][0]

    def some(levels):
        parts = []
        for level in levels:
            for head in range(HEADS):
                got, (active, block) = received[level], spots[level][head]
                c, at = cols(head), block_rows(block)
                scores = dot(scaled[at, c], got[head, :BLOCK], NT)
                parts.append((level, head, active, at, c, scores, dot(d[at, c], got[head, BLOCK : 2 * BLOCK], NT)))
        grads = []
        for level, head, active, at, c, scores, pull in parts:
            probs = jnp.exp(scores * SCALE - norm_cols[head, at, :])
            grads.append((probs * pull).astype(jnp.bfloat16))
        mores = [dot(grad, received[p[0]][p[1], :BLOCK], NN) for grad, p in zip(grads, parts)]
        sums = [0.0] * HEADS
        for more, (level, head, active, at, c, _, _) in zip(mores, parts):
            more = jnp.where(active, more, 0.0)
            added[level - 1, head] = more
            sums[head] = sums[head] + jnp.sum(q[at, c].astype(jnp.float32) * more, axis=0, keepdims=True)
        for head in range(HEADS):
            total[:, cols(head)] += sums[head]

    some((1, 2, 3, 4))
    partial[...] = jnp.broadcast_to((total[...] * SCALE)[None], partial.shape)


def add_keys(level, spots, got, first, gain, k, v, dk, dv):
    for head in range(HEADS):
        active, block = spots[head]
        c, at = cols(head), block_rows(block)
        query = scale_rows(got[head, :BLOCK], gain[:, c])
        if level in LATE:
            parts = first[head, 2 * BLOCK : 2 * BLOCK + PARTS]
            dout = jnp.concatenate([got[head, BLOCK:], first[head, 2 * BLOCK + PARTS :]], axis=0)
        else:
            parts, dout = got[head, 2 * BLOCK :], got[head, BLOCK : 2 * BLOCK]
        parts = parts.astype(jnp.float32)
        norm = parts[0:1] + parts[1:2] + parts[2:3]
        probs = jnp.exp(dot(k[at, c], query, NT) * SCALE - norm)
        grads = (probs * dot(v[at, c], dout, NT)).astype(jnp.bfloat16)
        dk[at, c] += jnp.where(active, dot(grads, query, NN), 0.0)
        dv[at, c] += jnp.where(active, dot(probs.astype(jnp.bfloat16), dout, NN), 0.0)


def most_kernel(offsets, gain, scaled, k, v, d, norm, dq_in, added, *refs):
    received, (grad_q, dk, dv, dq) = dict(zip(SOON, refs)), refs[len(SOON) :]
    for head in range(HEADS):
        c = cols(head)
        count = block_counts(offsets, head)
        query, key, value, dout = scaled[:, c], k[:, c], v[:, c], d[:, c]
        probs = jnp.exp(dot(key, query, NT) * SCALE - norm[head : head + 1, :])
        grads = (probs * dot(value, dout, NT)).astype(jnp.bfloat16)
        probs = probs.astype(jnp.bfloat16)
        for b in range(2):
            own, other = both_blocks(b)
            dk[own, c] = count[b] * dot(grads[own, own], query[own], NN) + dot(grads[own, other], query[other], NN)
            dv[own, c] = count[b] * dot(probs[own, own], dout[own], NN) + dot(probs[own, other], dout[other], NN)
    dq[...] = dq_in[...]

    def add_queries(level, spots):
        for head in range(HEADS):
            dq[block_rows(spots[head][1]), cols(head)] += added[level - 1, head]

    for_each_level(offsets, range(1, LEVELS), add_queries)
    grad_q[...] = (dq[...] * SCALE * gain[...]).astype(jnp.bfloat16)
    for_each_level(
        offsets, SOON, lambda level, spots: add_keys(level, spots, received[level], None, gain, k, v, dk, dv)
    )


def last_kernel(offsets, gain, k, v, dk_in, dv_in, *refs):
    got, first = dict(zip(LATE, refs)), dict(zip(LATE, refs[len(LATE) :]))
    grad_k, grad_v, dk, dv = refs[2 * len(LATE) :]
    dk[...] = dk_in[...]
    dv[...] = dv_in[...]
    for_each_level(
        offsets, LATE, lambda level, spots: add_keys(level, spots, got[level], first[level], gain, k, v, dk, dv)
    )
    grad_k[...] = (dk[...] * SCALE).astype(jnp.bfloat16)
    grad_v[...] = dv[...].astype(jnp.bfloat16)


def call(kernel, name, outs, in_specs, scratch=(), out_specs=None, aliases=None):
    return pl.pallas_call(
        kernel,
        name=name,
        out_shape=outs,
        in_specs=in_specs,
        out_specs=out_specs or [VMEM] * len(outs),
        scratch_shapes=list(scratch),
        input_output_aliases=aliases or {},
        compiler_params=pltpu.CompilerParams(vmem_limit_bytes=32 * 1024 * 1024),
    )


def in_hbm(array):
    return pltpu.with_memory_space_constraint(array, pltpu.HBM)


def swap(payloads):
    count, got = lax.axis_size("ctx"), {}
    for level, payload in payloads.items():
        half = 1 << (level - 1)
        got[level] = lax.ppermute(payload, "ctx", [(i, i ^ half) for i in range(count)])
    return got


def body(queries, keys, values, grad_out, log_norm, offsets, q_gain):
    q, k, v, d = queries[0], keys[0], values[0], grad_out[0]
    norm = log_norm[0]
    tokens, width = q.shape
    gain = q_gain.reshape(1, width)
    f32 = functools.partial(jax.ShapeDtypeStruct, dtype=jnp.float32)
    bf16 = functools.partial(jax.ShapeDtypeStruct, dtype=jnp.bfloat16)
    many = LEVELS - 1
    raw = pltpu.VMEM((tokens, width), jnp.bfloat16)
    *sent, norm, gain, table = call(
        pack_kernel,
        "pack",
        [bf16((HEADS, 2 * BLOCK + (PARTS + EARLY) * (level in LATE), HD)) for level in range(1, LEVELS)]
        + [bf16((HEADS, 2 * BLOCK + (-EARLY if level in LATE else PARTS), HD)) for level in range(1, LEVELS)]
        + [f32(norm.shape), f32(gain.shape), jax.ShapeDtypeStruct(offsets.shape, jnp.int32)],
        [HBM] * 7,
        [pltpu.SMEM(offsets.shape, jnp.int32), raw, raw, raw, raw, pltpu.SemaphoreType.DMA((8,))],
    )(*map(in_hbm, (offsets, k, v, q, d, norm, gain)))
    offsets = table
    second = dict(zip(range(1, LEVELS), sent[many:]))
    got_kv = swap({level: sent[level - 1] for level in ORDER})
    early = {level: second[level] for level in SOON}
    dq, norm_cols, scaled, partial, *passed = call(
        local_q_kernel,
        "local_q",
        [f32((tokens, width)), f32((HEADS, tokens, HD)), bf16((tokens, width)), f32((1, width))]
        + [bf16(p.shape) for p in early.values()],
        [SMEM] + [VMEM] * 6 + [ANY] * len(early),
        out_specs=[VMEM] * 4 + [ANY] * len(early),
        aliases={7 + i: 4 + i for i in range(len(early))},
    )(offsets, gain, q, k, v, d, norm, *early.values())
    got_qd = swap(dict(zip(early, passed)))
    axes = ("dp", "ctx")
    everyone = lax.axis_size(axes)
    late = [second[level] for level in LATE]
    added, partial, *late = call(
        query_kernel,
        "remote_q",
        [f32((many, HEADS, BLOCK, HD)), f32((everyone, 1, width))] + [bf16(p.shape) for p in late],
        [SMEM] + [VMEM] * 9 + [ANY] * len(late),
        [pltpu.VMEM((1, width), jnp.float32)],
        [VMEM] * 2 + [ANY] * len(late),
        {10 + i: 2 + i for i in range(len(late))},
    )(offsets, scaled, q, d, norm_cols, partial, *(got_kv[level] for level in ORDER), *late)
    got_qd.update(swap(dict(zip(LATE, late))))
    parts = lax.all_to_all(partial, axes, 0, 0, tiled=True)
    acc = pltpu.VMEM((tokens, width), jnp.float32)
    grad_q, dk, dv = call(
        most_kernel,
        "most_kv",
        [bf16((tokens, width)), f32((tokens, width)), f32((tokens, width))],
        [SMEM] + [VMEM] * (8 + len(SOON)),
        [acc],
    )(offsets, gain, scaled, k, v, d, norm, dq, added, *(got_qd[level] for level in SOON))
    grad_k, grad_v = call(
        last_kernel, "last_kv", [bf16((tokens, width))] * 2, [SMEM] + [VMEM] * (5 + 2 * len(LATE)), [acc, acc]
    )(offsets, gain, k, v, dk, dv, *(got_qd[level] for level in LATE), *(got_kv[level] for level in LATE))
    return (grad_q[None], grad_k[None], grad_v[None], jnp.sum(parts, axis=(0, 1)))


def solution(mesh):
    rows = P("dp", "ctx", None)
    in_specs = (rows, rows, rows, rows, P("dp", None, "ctx"), P(), P())
    out_specs = (rows, rows, rows, P())
    return jax.shard_map(body, mesh=mesh, in_specs=in_specs, out_specs=out_specs, check_vma=False)
```

```python
import functools

import jax
import jax.numpy as jnp
from jax import lax
from jax.experimental import pallas as pl
from jax.experimental.pallas import tpu as pltpu
from jax.sharding import PartitionSpec as P

BLOCK = 128
LEVELS = 5
HEADS = 2
HD = 128
SCALE = HD**-0.5
LATE, EARLY, PARTS = (4,), 16, 16

HBM = pl.BlockSpec(memory_space=pltpu.HBM)
ANY = pl.BlockSpec(memory_space=pl.ANY)
VMEM = pl.BlockSpec(memory_space=pltpu.VMEM)
SMEM = pl.BlockSpec(memory_space=pltpu.SMEM)
ORDER = (4,1,2,3)
SOON = (3,2,1,)
NT = (((1,), (1,)), ((), ()))
TN = (((0,), (0,)), ((), ()))
NN = (((1,), (0,)), ((), ()))


def dot(left, right, dims):
    return lax.dot_general(left, right, dims, preferred_element_type=jnp.float32)


def cols(head):
    return slice(head * HD, (head + 1) * HD)


def place(offsets, me, head, level):
    half = 1 << (level - 1)
    shift = offsets[head, level] & (2 * half - 1)
    return (me & (half - 1)) == (shift >> 1), shift & 1


def block_rows(block):
    return pl.ds(pl.multiple_of(block * BLOCK, BLOCK), BLOCK)


def scale_rows(rows, gain):
    return (rows.astype(jnp.float32) * gain).astype(jnp.bfloat16)


def split_norm(norm, head, block):
    whole = jnp.where(block == 0, norm[head : head + 1, :BLOCK], norm[head : head + 1, BLOCK:])
    high = whole.astype(jnp.bfloat16).astype(jnp.float32)
    rest = whole - high
    mid = rest.astype(jnp.bfloat16).astype(jnp.float32)
    low = rest - mid
    row = lax.broadcasted_iota(jnp.int32, (PARTS, BLOCK), 0)
    parts = jnp.where(row == 0, high, jnp.where(row == 1, mid, jnp.where(row == 2, low, 0.0)))
    return parts.astype(jnp.bfloat16)


def pack_kernel(offsets_in, k_in, v_in, d_in, norm_in, gain_in, q_in, *refs):
    firsts, (norm, gain, table, q, k, v, d), (offsets, sems) = refs[:4], refs[4:11], refs[11:]
    copies = []
    moves = ((offsets_in, offsets), (k_in, k), (v_in, v), (d_in, d))
    moves += ((norm_in, norm), (gain_in, gain), (offsets_in, table), (q_in, q))
    for i, (source, target) in enumerate(moves):
        copies.append(pltpu.make_async_copy(source, target, sems.at[i]))
        copies[-1].start()
    for copy in copies:
        copy.wait()
    for level in range(1, LEVELS):
        first = firsts[level - 1]
        for head in range(HEADS):
            block, c = offsets[head, level] & 1, cols(head)
            at = block_rows(block)
            first[head, :BLOCK] = k[at, c]
            first[head, BLOCK : 2 * BLOCK] = v[at, c]
            if level in LATE:
                start = pl.multiple_of(block * BLOCK, BLOCK)
                first[head, 2 * BLOCK : 2 * BLOCK + PARTS] = split_norm(norm, head, block)
                first[head, 2 * BLOCK + PARTS :] = d[pl.ds(start + BLOCK - EARLY, EARLY), c]


def pack_second(offsets, q, d, norm, seconds):
    for level in range(1, LEVELS):
        second = seconds[level - 1]
        for head in range(HEADS):
            block, c = offsets[head, level] & 1, cols(head)
            at = block_rows(block)
            second[head, :BLOCK] = q[at, c]
            if level in LATE:
                start = pl.multiple_of(block * BLOCK, BLOCK)
                second[head, BLOCK:] = d[pl.ds(start, BLOCK - EARLY), c]
            else:
                second[head, BLOCK : 2 * BLOCK] = d[at, c]
                second[head, 2 * BLOCK :] = split_norm(norm, head, block)


def block_counts(offsets, head):
    me = lax.axis_index("ctx")
    count = [jnp.float32(1.0), jnp.float32(1.0)]
    for level in range(1, LEVELS):
        active, block = place(offsets, me, head, level)
        for b in range(2):
            count[b] = count[b] + jnp.where(active & (block == b), 1.0, 0.0)
    return count


def both_blocks(b):
    return slice(b * BLOCK, (b + 1) * BLOCK), slice((1 - b) * BLOCK, (2 - b) * BLOCK)


def local_q_kernel(offsets, gain, q, k, v, d, norm, dq, norm_cols, scaled, partial, *seconds):
    pack_second(offsets, q, d, norm, seconds)
    for head in range(HEADS):
        c = cols(head)
        count = block_counts(offsets, head)
        query, key, value, dout = scale_rows(q[:, c], gain[:, c]), k[:, c], v[:, c], d[:, c]
        scaled[:, c] = query
        column = jnp.transpose(jnp.broadcast_to(norm[head : head + 1, :], (BLOCK, 2 * BLOCK)))
        norm_cols[head] = column
        probs = jnp.exp(dot(query, key, NT) * SCALE - jnp.concatenate([column, column], axis=1))
        grads = (probs * dot(dout, value, NT)).astype(jnp.bfloat16)
        for b in range(2):
            own, other = both_blocks(b)
            dq[own, c] = count[b] * dot(grads[own, own], key[own], NN) + dot(grads[own, other], key[other], NN)
        partial[:, c] = jnp.sum(q[:, c].astype(jnp.float32) * dq[:, c], axis=0, keepdims=True)


def for_each_level(offsets, levels, fn):
    me = lax.axis_index("ctx")
    for level in levels:
        spots = [place(offsets, me, head, level) for head in range(HEADS)]

        def both(level=level, spots=spots):
            fn(level, spots)

        if level == 1:
            both()
        else:
            pl.when(spots[0][0] | spots[1][0])(both)


def query_kernel(offsets, scaled, q, d, norm_cols, partial_in, r1, r2, r3, r4, *refs):
    added, partial, total = refs[len(LATE)], refs[len(LATE) + 1], refs[-1]
    received = dict(zip(ORDER, (r1, r2, r3, r4)))
    total[...] = partial_in[...]

    me = lax.axis_index("ctx")
    spots = {level: [place(offsets, me, head, level) for head in range(HEADS)] for level in range(1, LEVELS)}

    def any_active(level):
        return spots[level][0][0] | spots[level][1][0]

    def some(levels):
        parts = []
        for level in levels:
            for head in range(HEADS):
                got, (active, block) = received[level], spots[level][head]
                c, at = cols(head), block_rows(block)
                scores = dot(scaled[at, c], got[head, :BLOCK], NT)
                parts.append((level, head, active, at, c, scores, dot(d[at, c], got[head, BLOCK : 2 * BLOCK], NT)))
        grads = []
        for level, head, active, at, c, scores, pull in parts:
            probs = jnp.exp(scores * SCALE - norm_cols[head, at, :])
            grads.append((probs * pull).astype(jnp.bfloat16))
        mores = [dot(grad, received[p[0]][p[1], :BLOCK], NN) for grad, p in zip(grads, parts)]
        sums = [0.0] * HEADS
        for more, (level, head, active, at, c, _, _) in zip(mores, parts):
            more = jnp.where(active, more, 0.0)
            added[level - 1, head] = more
            sums[head] = sums[head] + jnp.sum(q[at, c].astype(jnp.float32) * more, axis=0, keepdims=True)
        for head in range(HEADS):
            total[:, cols(head)] += sums[head]

    some((1, 2, 3, 4))
    partial[...] = jnp.broadcast_to((total[...] * SCALE)[None], partial.shape)


def add_keys(level, spots, got, first, gain, k, v, dk, dv):
    for head in range(HEADS):
        active, block = spots[head]
        c, at = cols(head), block_rows(block)
        query = scale_rows(got[head, :BLOCK], gain[:, c])
        if level in LATE:
            parts = first[head, 2 * BLOCK : 2 * BLOCK + PARTS]
            dout = jnp.concatenate([got[head, BLOCK:], first[head, 2 * BLOCK + PARTS :]], axis=0)
        else:
            parts, dout = got[head, 2 * BLOCK :], got[head, BLOCK : 2 * BLOCK]
        parts = parts.astype(jnp.float32)
        norm = parts[0:1] + parts[1:2] + parts[2:3]
        probs = jnp.exp(dot(k[at, c], query, NT) * SCALE - norm)
        grads = (probs * dot(v[at, c], dout, NT)).astype(jnp.bfloat16)
        dk[at, c] += jnp.where(active, dot(grads, query, NN), 0.0)
        dv[at, c] += jnp.where(active, dot(probs.astype(jnp.bfloat16), dout, NN), 0.0)


def most_kernel(offsets, gain, scaled, k, v, d, norm, dq_in, added, *refs):
    received, (grad_q, dk, dv, dq) = dict(zip(SOON, refs)), refs[len(SOON) :]
    for head in range(HEADS):
        c = cols(head)
        count = block_counts(offsets, head)
        query, key, value, dout = scaled[:, c], k[:, c], v[:, c], d[:, c]
        probs = jnp.exp(dot(key, query, NT) * SCALE - norm[head : head + 1, :])
        grads = (probs * dot(value, dout, NT)).astype(jnp.bfloat16)
        probs = probs.astype(jnp.bfloat16)
        for b in range(2):
            own, other = both_blocks(b)
            dk[own, c] = count[b] * dot(grads[own, own], query[own], NN) + dot(grads[own, other], query[other], NN)
            dv[own, c] = count[b] * dot(probs[own, own], dout[own], NN) + dot(probs[own, other], dout[other], NN)
    dq[...] = dq_in[...]

    def add_queries(level, spots):
        for head in range(HEADS):
            dq[block_rows(spots[head][1]), cols(head)] += added[level - 1, head]

    for_each_level(offsets, range(1, LEVELS), add_queries)
    grad_q[...] = (dq[...] * SCALE * gain[...]).astype(jnp.bfloat16)
    for_each_level(
        offsets, SOON, lambda level, spots: add_keys(level, spots, received[level], None, gain, k, v, dk, dv)
    )


def last_kernel(offsets, gain, k, v, dk_in, dv_in, *refs):
    got, first = dict(zip(LATE, refs)), dict(zip(LATE, refs[len(LATE) :]))
    grad_k, grad_v, dk, dv = refs[2 * len(LATE) :]
    dk[...] = dk_in[...]
    dv[...] = dv_in[...]
    for_each_level(
        offsets, LATE, lambda level, spots: add_keys(level, spots, got[level], first[level], gain, k, v, dk, dv)
    )
    grad_k[...] = (dk[...] * SCALE).astype(jnp.bfloat16)
    grad_v[...] = dv[...].astype(jnp.bfloat16)


def call(kernel, name, outs, in_specs, scratch=(), out_specs=None, aliases=None):
    return pl.pallas_call(
        kernel,
        name=name,
        out_shape=outs,
        in_specs=in_specs,
        out_specs=out_specs or [VMEM] * len(outs),
        scratch_shapes=list(scratch),
        input_output_aliases=aliases or {},
        compiler_params=pltpu.CompilerParams(vmem_limit_bytes=32 * 1024 * 1024),
    )


def in_hbm(array):
    return pltpu.with_memory_space_constraint(array, pltpu.HBM)


def swap(payloads):
    count, got = lax.axis_size("ctx"), {}
    for level, payload in payloads.items():
        half = 1 << (level - 1)
        got[level] = lax.ppermute(payload, "ctx", [(i, i ^ half) for i in range(count)])
    return got


def body(queries, keys, values, grad_out, log_norm, offsets, q_gain):
    q, k, v, d = queries[0], keys[0], values[0], grad_out[0]
    norm = log_norm[0]
    tokens, width = q.shape
    gain = q_gain.reshape(1, width)
    f32 = functools.partial(jax.ShapeDtypeStruct, dtype=jnp.float32)
    bf16 = functools.partial(jax.ShapeDtypeStruct, dtype=jnp.bfloat16)
    many = LEVELS - 1
    *firsts, norm, gain, table, q, k, v, d = call(
        pack_kernel,
        "pack",
        [bf16((HEADS, 2 * BLOCK + (PARTS + EARLY) * (level in LATE), HD)) for level in range(1, LEVELS)]
        + [f32(norm.shape), f32(gain.shape), jax.ShapeDtypeStruct(offsets.shape, jnp.int32)]
        + [bf16((tokens, width))] * 4,
        [HBM] * 7,
        [pltpu.SMEM(offsets.shape, jnp.int32), pltpu.SemaphoreType.DMA((8,))],
    )(*map(in_hbm, (offsets, k, v, d, norm, gain, q)))
    offsets = table
    got_kv = swap({level: firsts[level - 1] for level in ORDER})
    dq, norm_cols, scaled, partial, *second = call(
        local_q_kernel,
        "local_q",
        [f32((tokens, width)), f32((HEADS, tokens, HD)), bf16((tokens, width)), f32((1, width))]
        + [bf16((HEADS, 2 * BLOCK + (-EARLY if level in LATE else PARTS), HD)) for level in range(1, LEVELS)],
        [SMEM] + [VMEM] * 6,
    )(offsets, gain, q, k, v, d, norm)
    got_qd = swap({level: second[level - 1] for level in SOON})
    axes = ("dp", "ctx")
    everyone = lax.axis_size(axes)
    late = [second[level - 1] for level in LATE]
    added, partial, *late = call(
        query_kernel,
        "remote_q",
        [f32((many, HEADS, BLOCK, HD)), f32((everyone, 1, width))] + [bf16(p.shape) for p in late],
        [SMEM] + [VMEM] * 9 + [ANY] * len(late),
        [pltpu.VMEM((1, width), jnp.float32)],
        [VMEM] * 2 + [ANY] * len(late),
        {10 + i: 2 + i for i in range(len(late))},
    )(offsets, scaled, q, d, norm_cols, partial, *(got_kv[level] for level in ORDER), *late)
    got_qd.update(swap(dict(zip(LATE, late))))
    parts = lax.all_to_all(partial, axes, 0, 0, tiled=True)
    acc = pltpu.VMEM((tokens, width), jnp.float32)
    grad_q, dk, dv = call(
        most_kernel,
        "most_kv",
        [bf16((tokens, width)), f32((tokens, width)), f32((tokens, width))],
        [SMEM] + [VMEM] * (8 + len(SOON)),
        [acc],
    )(offsets, gain, scaled, k, v, d, norm, dq, added, *(got_qd[level] for level in SOON))
    grad_k, grad_v = call(
        last_kernel, "last_kv", [bf16((tokens, width))] * 2, [SMEM] + [VMEM] * (5 + 2 * len(LATE)), [acc, acc]
    )(offsets, gain, k, v, dk, dv, *(got_qd[level] for level in LATE), *(got_kv[level] for level in LATE))
    return (grad_q[None], grad_k[None], grad_v[None], jnp.sum(parts, axis=(0, 1)))


def solution(mesh):
    rows = P("dp", "ctx", None)
    in_specs = (rows, rows, rows, rows, P("dp", None, "ctx"), P(), P())
    out_specs = (rows, rows, rows, P())
    return jax.shard_map(body, mesh=mesh, in_specs=in_specs, out_specs=out_specs, check_vma=False)
```

```python
import functools

import jax
import jax.numpy as jnp
from jax import lax
from jax.experimental import pallas as pl
from jax.experimental.pallas import tpu as pltpu
from jax.sharding import PartitionSpec as P

BLOCK = 128
LEVELS = 5
HEADS = 2
HD = 128
SCALE = HD**-0.5
LATE, EARLY, PARTS = (4,), 16, 16

HBM = pl.BlockSpec(memory_space=pltpu.HBM)
ANY = pl.BlockSpec(memory_space=pl.ANY)
VMEM = pl.BlockSpec(memory_space=pltpu.VMEM)
SMEM = pl.BlockSpec(memory_space=pltpu.SMEM)
ORDER = (4,1,2,3)
SOON = (3,2,1,)
NT = (((1,), (1,)), ((), ()))
TN = (((0,), (0,)), ((), ()))
NN = (((1,), (0,)), ((), ()))


def dot(left, right, dims):
    return lax.dot_general(left, right, dims, preferred_element_type=jnp.float32)


def cols(head):
    return slice(head * HD, (head + 1) * HD)


def place(offsets, me, head, level):
    half = 1 << (level - 1)
    shift = offsets[head, level] & (2 * half - 1)
    return (me & (half - 1)) == (shift >> 1), shift & 1


def block_rows(block):
    return pl.ds(pl.multiple_of(block * BLOCK, BLOCK), BLOCK)


def scale_rows(rows, gain):
    return (rows.astype(jnp.float32) * gain).astype(jnp.bfloat16)


def split_norm(norm, head, block):
    whole = jnp.where(block == 0, norm[head : head + 1, :BLOCK], norm[head : head + 1, BLOCK:])
    high = whole.astype(jnp.bfloat16).astype(jnp.float32)
    rest = whole - high
    mid = rest.astype(jnp.bfloat16).astype(jnp.float32)
    low = rest - mid
    row = lax.broadcasted_iota(jnp.int32, (PARTS, BLOCK), 0)
    parts = jnp.where(row == 0, high, jnp.where(row == 1, mid, jnp.where(row == 2, low, 0.0)))
    return parts.astype(jnp.bfloat16)


def pack_kernel(offsets_in, k_in, v_in, d_in, norm_in, gain_in, q_in, *refs):
    firsts, (norm, gain, table, q, k, v, d), (offsets, sems) = refs[:4], refs[4:11], refs[11:]
    copies = []
    moves = ((offsets_in, offsets), (k_in, k), (v_in, v), (d_in, d))
    moves += ((norm_in, norm), (gain_in, gain), (offsets_in, table), (q_in, q))
    for i, (source, target) in enumerate(moves):
        copies.append(pltpu.make_async_copy(source, target, sems.at[i]))
        copies[-1].start()
    for copy in copies:
        copy.wait()
    for level in range(1, LEVELS):
        first = firsts[level - 1]
        for head in range(HEADS):
            block, c = offsets[head, level] & 1, cols(head)
            at = block_rows(block)
            first[head, :BLOCK] = k[at, c]
            first[head, BLOCK : 2 * BLOCK] = v[at, c]
            if level in LATE:
                start = pl.multiple_of(block * BLOCK, BLOCK)
                first[head, 2 * BLOCK : 2 * BLOCK + PARTS] = split_norm(norm, head, block)
                first[head, 2 * BLOCK + PARTS :] = d[pl.ds(start + BLOCK - EARLY, EARLY), c]


def pack_second(offsets, q, d, norm, seconds):
    for level in range(1, LEVELS):
        second = seconds[level - 1]
        for head in range(HEADS):
            block, c = offsets[head, level] & 1, cols(head)
            at = block_rows(block)
            second[head, :BLOCK] = q[at, c]
            if level in LATE:
                start = pl.multiple_of(block * BLOCK, BLOCK)
                second[head, BLOCK:] = d[pl.ds(start, BLOCK - EARLY), c]
            else:
                second[head, BLOCK : 2 * BLOCK] = d[at, c]
                second[head, 2 * BLOCK :] = split_norm(norm, head, block)


def block_counts(offsets, head):
    me = lax.axis_index("ctx")
    count = [jnp.float32(1.0), jnp.float32(1.0)]
    for level in range(1, LEVELS):
        active, block = place(offsets, me, head, level)
        for b in range(2):
            count[b] = count[b] + jnp.where(active & (block == b), 1.0, 0.0)
    return count


def both_blocks(b):
    return slice(b * BLOCK, (b + 1) * BLOCK), slice((1 - b) * BLOCK, (2 - b) * BLOCK)


def local_q_kernel(offsets, gain, q, k, v, d, norm, dq, scaled, partial, picked, picked_norm, taking, *seconds):
    pack_second(offsets, q, d, norm, seconds)
    me = lax.axis_index("ctx")
    row = lax.broadcasted_iota(jnp.int32, taking.shape, 0)
    flags = jnp.zeros(taking.shape, jnp.float32)
    parts = []
    for head in range(HEADS):
        c = cols(head)
        query, key = scale_rows(q[:, c], gain[:, c]), k[:, c]
        scaled[:, c] = query
        parts.append((c, key, dot(query, key, NT), dot(d[:, c], v[:, c], NT)))
    for head, (c, key, scores, pull) in enumerate(parts):
        column = jnp.transpose(jnp.broadcast_to(norm[head : head + 1, :], (BLOCK, 2 * BLOCK)))
        for level in range(1, LEVELS):
            active, block = place(offsets, me, head, level)
            at = block_rows(block)
            picked_norm[level - 1, head] = jnp.where(block == 0, column[:BLOCK], column[BLOCK:])
            for i, source in enumerate((scaled, q, d)):
                picked[i, level - 1, head] = source[at, c]
            flags = jnp.where((row == HEADS * (level - 1) + head) & active, 1.0, flags)
        probs = jnp.exp(scores * SCALE - jnp.concatenate([column, column], axis=1))
        parts[head] = (c, key, (probs * pull).astype(jnp.bfloat16))
    for head, (c, key, grads) in enumerate(parts):
        count = block_counts(offsets, head)
        sums = 0.0
        for b in range(2):
            own, other = both_blocks(b)
            more = count[b] * dot(grads[own, own], key[own], NN) + dot(grads[own, other], key[other], NN)
            dq[own, c] = more
            sums = sums + jnp.sum(q[own, c].astype(jnp.float32) * more, axis=0, keepdims=True)
        partial[:, c] = sums
    taking[...] = flags


def for_each_level(offsets, levels, fn):
    me = lax.axis_index("ctx")
    for level in levels:
        spots = [place(offsets, me, head, level) for head in range(HEADS)]

        def both(level=level, spots=spots):
            fn(level, spots)

        if level == 1:
            both()
        else:
            pl.when(spots[0][0] | spots[1][0])(both)


def query_kernel(picked, picked_norm, taking, partial_in, r1, r2, r3, r4, *refs):
    added, partial = refs[len(LATE)], refs[len(LATE) + 1]
    received = dict(zip(ORDER, (r1, r2, r3, r4)))
    spots = [(level, head) for level in range(1, LEVELS) for head in range(HEADS)]
    products = []
    for level, head in spots:
        got, n = received[level], level - 1
        scores = dot(picked[0, n, head], got[head, :BLOCK], NT)
        products.append((scores, dot(picked[2, n, head], got[head, BLOCK : 2 * BLOCK], NT)))
    grads = []
    for (level, head), (scores, pull) in zip(spots, products):
        probs = jnp.exp(scores * SCALE - picked_norm[level - 1, head])
        grads.append((probs * pull).astype(jnp.bfloat16))
    mores = [dot(grad, received[level][head, :BLOCK], NN) for (level, head), grad in zip(spots, grads)]
    sums = [partial_in[:, cols(head)] for head in range(HEADS)]
    for (level, head), more in zip(spots, mores):
        n = level - 1
        more = jnp.where(taking[HEADS * n + head : HEADS * n + head + 1, :] > 0.0, more, 0.0)
        added[n, head] = more
        sums[head] = sums[head] + jnp.sum(picked[1, n, head].astype(jnp.float32) * more, axis=0, keepdims=True)
    total = jnp.concatenate(sums, axis=1) * SCALE
    partial[...] = jnp.broadcast_to(total[None], partial.shape)


def add_keys(level, spots, got, first, gain, k, v, dk, dv):
    for head in range(HEADS):
        active, block = spots[head]
        c, at = cols(head), block_rows(block)
        query = scale_rows(got[head, :BLOCK], gain[:, c])
        if level in LATE:
            parts = first[head, 2 * BLOCK : 2 * BLOCK + PARTS]
            dout = jnp.concatenate([got[head, BLOCK:], first[head, 2 * BLOCK + PARTS :]], axis=0)
        else:
            parts, dout = got[head, 2 * BLOCK :], got[head, BLOCK : 2 * BLOCK]
        parts = parts.astype(jnp.float32)
        norm = parts[0:1] + parts[1:2] + parts[2:3]
        probs = jnp.exp(dot(k[at, c], query, NT) * SCALE - norm)
        grads = (probs * dot(v[at, c], dout, NT)).astype(jnp.bfloat16)
        dk[at, c] += jnp.where(active, dot(grads, query, NN), 0.0)
        dv[at, c] += jnp.where(active, dot(probs.astype(jnp.bfloat16), dout, NN), 0.0)


def most_kernel(offsets, gain, scaled, k, v, d, norm, dq_in, added, *refs):
    received, (grad_q, dk, dv, dq) = dict(zip(SOON, refs)), refs[len(SOON) :]
    for head in range(HEADS):
        c = cols(head)
        count = block_counts(offsets, head)
        query, key, value, dout = scaled[:, c], k[:, c], v[:, c], d[:, c]
        probs = jnp.exp(dot(key, query, NT) * SCALE - norm[head : head + 1, :])
        grads = (probs * dot(value, dout, NT)).astype(jnp.bfloat16)
        probs = probs.astype(jnp.bfloat16)
        for b in range(2):
            own, other = both_blocks(b)
            dk[own, c] = count[b] * dot(grads[own, own], query[own], NN) + dot(grads[own, other], query[other], NN)
            dv[own, c] = count[b] * dot(probs[own, own], dout[own], NN) + dot(probs[own, other], dout[other], NN)
    dq[...] = dq_in[...]

    def add_queries(level, spots):
        for head in range(HEADS):
            dq[block_rows(spots[head][1]), cols(head)] += added[level - 1, head]

    for_each_level(offsets, range(1, LEVELS), add_queries)
    grad_q[...] = (dq[...] * SCALE * gain[...]).astype(jnp.bfloat16)
    for_each_level(
        offsets, SOON, lambda level, spots: add_keys(level, spots, received[level], None, gain, k, v, dk, dv)
    )


def last_kernel(offsets, gain, k, v, dk_in, dv_in, *refs):
    got, first = dict(zip(LATE, refs)), dict(zip(LATE, refs[len(LATE) :]))
    grad_k, grad_v, dk, dv = refs[2 * len(LATE) :]
    dk[...] = dk_in[...]
    dv[...] = dv_in[...]
    for_each_level(
        offsets, LATE, lambda level, spots: add_keys(level, spots, got[level], first[level], gain, k, v, dk, dv)
    )
    grad_k[...] = (dk[...] * SCALE).astype(jnp.bfloat16)
    grad_v[...] = dv[...].astype(jnp.bfloat16)


def call(kernel, name, outs, in_specs, scratch=(), out_specs=None, aliases=None):
    return pl.pallas_call(
        kernel,
        name=name,
        out_shape=outs,
        in_specs=in_specs,
        out_specs=out_specs or [VMEM] * len(outs),
        scratch_shapes=list(scratch),
        input_output_aliases=aliases or {},
        compiler_params=pltpu.CompilerParams(vmem_limit_bytes=32 * 1024 * 1024),
    )


def in_hbm(array):
    return pltpu.with_memory_space_constraint(array, pltpu.HBM)


def swap(payloads):
    count, got = lax.axis_size("ctx"), {}
    for level, payload in payloads.items():
        half = 1 << (level - 1)
        got[level] = lax.ppermute(payload, "ctx", [(i, i ^ half) for i in range(count)])
    return got


def body(queries, keys, values, grad_out, log_norm, offsets, q_gain):
    q, k, v, d = queries[0], keys[0], values[0], grad_out[0]
    norm = log_norm[0]
    tokens, width = q.shape
    gain = q_gain.reshape(1, width)
    f32 = functools.partial(jax.ShapeDtypeStruct, dtype=jnp.float32)
    bf16 = functools.partial(jax.ShapeDtypeStruct, dtype=jnp.bfloat16)
    many = LEVELS - 1
    *firsts, norm, gain, table, q, k, v, d = call(
        pack_kernel,
        "pack",
        [bf16((HEADS, 2 * BLOCK + (PARTS + EARLY) * (level in LATE), HD)) for level in range(1, LEVELS)]
        + [f32(norm.shape), f32(gain.shape), jax.ShapeDtypeStruct(offsets.shape, jnp.int32)]
        + [bf16((tokens, width))] * 4,
        [HBM] * 7,
        [pltpu.SMEM(offsets.shape, jnp.int32), pltpu.SemaphoreType.DMA((8,))],
    )(*map(in_hbm, (offsets, k, v, d, norm, gain, q)))
    offsets = table
    got_kv = swap({level: firsts[level - 1] for level in ORDER})
    dq, scaled, partial, *picks, s1, s2, s3, s4 = call(
        local_q_kernel,
        "local_q",
        [f32((tokens, width)), bf16((tokens, width)), f32((1, width))]
        + [bf16((3, many, HEADS, BLOCK, HD)), f32((many, HEADS, BLOCK, HD)), f32((many * HEADS, HD))]
        + [bf16((HEADS, 2 * BLOCK + (-EARLY if level in LATE else PARTS), HD)) for level in range(1, LEVELS)],
        [SMEM] + [VMEM] * 6,
    )(offsets, gain, q, k, v, d, norm)
    second = (s1, s2, s3, s4)
    got_qd = swap({level: second[level - 1] for level in SOON})
    axes = ("dp", "ctx")
    everyone = lax.axis_size(axes)
    late = [second[level - 1] for level in LATE]
    added, partial, *late = call(
        query_kernel,
        "remote_q",
        [f32((many, HEADS, BLOCK, HD)), f32((everyone, 1, width))] + [bf16(p.shape) for p in late],
        [VMEM] * 8 + [ANY] * len(late),
        (),
        [VMEM] * 2 + [ANY] * len(late),
        {8 + i: 2 + i for i in range(len(late))},
    )(*picks, partial, *(got_kv[level] for level in ORDER), *late)
    got_qd.update(swap(dict(zip(LATE, late))))
    parts = lax.all_to_all(partial, axes, 0, 0, tiled=True)
    acc = pltpu.VMEM((tokens, width), jnp.float32)
    grad_q, dk, dv = call(
        most_kernel,
        "most_kv",
        [bf16((tokens, width)), f32((tokens, width)), f32((tokens, width))],
        [SMEM] + [VMEM] * (8 + len(SOON)),
        [acc],
    )(offsets, gain, scaled, k, v, d, norm, dq, added, *(got_qd[level] for level in SOON))
    grad_k, grad_v = call(
        last_kernel, "last_kv", [bf16((tokens, width))] * 2, [SMEM] + [VMEM] * (5 + 2 * len(LATE)), [acc, acc]
    )(offsets, gain, k, v, dk, dv, *(got_qd[level] for level in LATE), *(got_kv[level] for level in LATE))
    return (grad_q[None], grad_k[None], grad_v[None], jnp.sum(parts, axis=(0, 1)))


def solution(mesh):
    rows = P("dp", "ctx", None)
    in_specs = (rows, rows, rows, rows, P("dp", None, "ctx"), P(), P())
    out_specs = (rows, rows, rows, P())
    return jax.shard_map(body, mesh=mesh, in_specs=in_specs, out_specs=out_specs, check_vma=False)
```

```python
import functools

import jax
import jax.numpy as jnp
from jax import lax
from jax.experimental import pallas as pl
from jax.experimental.pallas import tpu as pltpu
from jax.sharding import PartitionSpec as P

BLOCK = 128
LEVELS = 5
HEADS = 2
HD = 128
SCALE = HD**-0.5
LATE, EARLY, PARTS = (4,), 16, 16

HBM = pl.BlockSpec(memory_space=pltpu.HBM)
ANY = pl.BlockSpec(memory_space=pl.ANY)
VMEM = pl.BlockSpec(memory_space=pltpu.VMEM)
SMEM = pl.BlockSpec(memory_space=pltpu.SMEM)
ORDER = (4,1,2,3)
SOON = (3,2,1,)
NT = (((1,), (1,)), ((), ()))
TN = (((0,), (0,)), ((), ()))
NN = (((1,), (0,)), ((), ()))


def dot(left, right, dims):
    return lax.dot_general(left, right, dims, preferred_element_type=jnp.float32)


def cols(head):
    return slice(head * HD, (head + 1) * HD)


def place(offsets, me, head, level):
    half = 1 << (level - 1)
    shift = offsets[head, level] & (2 * half - 1)
    return (me & (half - 1)) == (shift >> 1), shift & 1


def block_rows(block):
    return pl.ds(pl.multiple_of(block * BLOCK, BLOCK), BLOCK)


def scale_rows(rows, gain):
    return (rows.astype(jnp.float32) * gain).astype(jnp.bfloat16)


def split_norm(norm, head, block):
    whole = jnp.where(block == 0, norm[head : head + 1, :BLOCK], norm[head : head + 1, BLOCK:])
    high = whole.astype(jnp.bfloat16).astype(jnp.float32)
    rest = whole - high
    mid = rest.astype(jnp.bfloat16).astype(jnp.float32)
    low = rest - mid
    row = lax.broadcasted_iota(jnp.int32, (PARTS, BLOCK), 0)
    parts = jnp.where(row == 0, high, jnp.where(row == 1, mid, jnp.where(row == 2, low, 0.0)))
    return parts.astype(jnp.bfloat16)


def pack_kernel(offsets_in, k_in, v_in, d_in, norm_in, gain_in, q_in, *refs):
    firsts, (norm, gain, table, q, k, v, d), (offsets, sems) = refs[:4], refs[4:11], refs[11:]
    copies = []
    moves = ((offsets_in, offsets), (k_in, k), (v_in, v), (d_in, d))
    moves += ((norm_in, norm), (gain_in, gain), (offsets_in, table), (q_in, q))
    for i, (source, target) in enumerate(moves):
        copies.append(pltpu.make_async_copy(source, target, sems.at[i]))
        copies[-1].start()
    for copy in copies[:3]:
        copy.wait()
    for level in sorted(range(1, LEVELS), key=LATE.count):
        if level == LATE[0]:
            for copy in copies[3:]:
                copy.wait()
        first = firsts[level - 1]
        for head in range(HEADS):
            block, c = offsets[head, level] & 1, cols(head)
            at = block_rows(block)
            first[head, :BLOCK] = k[at, c]
            first[head, BLOCK : 2 * BLOCK] = v[at, c]
            if level in LATE:
                start = pl.multiple_of(block * BLOCK, BLOCK)
                first[head, 2 * BLOCK : 2 * BLOCK + PARTS] = split_norm(norm, head, block)
                first[head, 2 * BLOCK + PARTS :] = d[pl.ds(start + BLOCK - EARLY, EARLY), c]


def pack_second(offsets, q, d, norm, seconds):
    for level in range(1, LEVELS):
        second = seconds[level - 1]
        for head in range(HEADS):
            block, c = offsets[head, level] & 1, cols(head)
            at = block_rows(block)
            second[head, :BLOCK] = q[at, c]
            if level in LATE:
                start = pl.multiple_of(block * BLOCK, BLOCK)
                second[head, BLOCK:] = d[pl.ds(start, BLOCK - EARLY), c]
            else:
                second[head, BLOCK : 2 * BLOCK] = d[at, c]
                second[head, 2 * BLOCK :] = split_norm(norm, head, block)


def block_counts(offsets, head):
    me = lax.axis_index("ctx")
    count = [jnp.float32(1.0), jnp.float32(1.0)]
    for level in range(1, LEVELS):
        active, block = place(offsets, me, head, level)
        for b in range(2):
            count[b] = count[b] + jnp.where(active & (block == b), 1.0, 0.0)
    return count


def both_blocks(b):
    return slice(b * BLOCK, (b + 1) * BLOCK), slice((1 - b) * BLOCK, (2 - b) * BLOCK)


def local_q_kernel(offsets, gain, q, k, v, d, norm, dq, scaled, partial, picked, picked_norm, taking, *seconds):
    pack_second(offsets, q, d, norm, seconds)
    me = lax.axis_index("ctx")
    row = lax.broadcasted_iota(jnp.int32, taking.shape, 0)
    flags = jnp.zeros(taking.shape, jnp.float32)
    parts = []
    for head in range(HEADS):
        c = cols(head)
        query, key = scale_rows(q[:, c], gain[:, c]), k[:, c]
        scaled[:, c] = query
        parts.append((c, key, dot(query, key, NT), dot(d[:, c], v[:, c], NT)))
    for head, (c, key, scores, pull) in enumerate(parts):
        column = jnp.transpose(jnp.broadcast_to(norm[head : head + 1, :], (BLOCK, 2 * BLOCK)))
        for level in range(1, LEVELS):
            active, block = place(offsets, me, head, level)
            at = block_rows(block)
            picked_norm[level - 1, head] = jnp.where(block == 0, column[:BLOCK], column[BLOCK:])
            for i, source in enumerate((scaled, q, d)):
                picked[i, level - 1, head] = source[at, c]
            flags = jnp.where((row == HEADS * (level - 1) + head) & active, 1.0, flags)
        probs = jnp.exp(scores * SCALE - jnp.concatenate([column, column], axis=1))
        parts[head] = (c, key, (probs * pull).astype(jnp.bfloat16))
    for head, (c, key, grads) in enumerate(parts):
        count = block_counts(offsets, head)
        sums = 0.0
        for b in range(2):
            own, other = both_blocks(b)
            more = count[b] * dot(grads[own, own], key[own], NN) + dot(grads[own, other], key[other], NN)
            dq[own, c] = more
            sums = sums + jnp.sum(q[own, c].astype(jnp.float32) * more, axis=0, keepdims=True)
        partial[:, c] = sums
    taking[...] = flags


def for_each_level(offsets, levels, fn):
    me = lax.axis_index("ctx")
    for level in levels:
        spots = [place(offsets, me, head, level) for head in range(HEADS)]

        def both(level=level, spots=spots):
            fn(level, spots)

        if level == 1:
            both()
        else:
            pl.when(spots[0][0] | spots[1][0])(both)


def query_kernel(picked, picked_norm, taking, partial_in, r1, r2, r3, r4, *refs):
    added, partial = refs[len(LATE)], refs[len(LATE) + 1]
    received = dict(zip(ORDER, (r1, r2, r3, r4)))
    spots = [(level, head) for level in range(1, LEVELS) for head in range(HEADS)]
    products = []
    for level, head in spots:
        got, n = received[level], level - 1
        scores = dot(picked[0, n, head], got[head, :BLOCK], NT)
        products.append((scores, dot(picked[2, n, head], got[head, BLOCK : 2 * BLOCK], NT)))
    grads = []
    for (level, head), (scores, pull) in zip(spots, products):
        probs = jnp.exp(scores * SCALE - picked_norm[level - 1, head])
        grads.append((probs * pull).astype(jnp.bfloat16))
    mores = [dot(grad, received[level][head, :BLOCK], NN) for (level, head), grad in zip(spots, grads)]
    sums = [partial_in[:, cols(head)] for head in range(HEADS)]
    for (level, head), more in zip(spots, mores):
        n = level - 1
        more = jnp.where(taking[HEADS * n + head : HEADS * n + head + 1, :] > 0.0, more, 0.0)
        added[n, head] = more
        sums[head] = sums[head] + jnp.sum(picked[1, n, head].astype(jnp.float32) * more, axis=0, keepdims=True)
    total = jnp.concatenate(sums, axis=1) * SCALE
    partial[...] = jnp.broadcast_to(total[None], partial.shape)


def add_keys(level, spots, got, first, gain, k, v, dk, dv):
    for head in range(HEADS):
        active, block = spots[head]
        c, at = cols(head), block_rows(block)
        query = scale_rows(got[head, :BLOCK], gain[:, c])
        if level in LATE:
            parts = first[head, 2 * BLOCK : 2 * BLOCK + PARTS]
            dout = jnp.concatenate([got[head, BLOCK:], first[head, 2 * BLOCK + PARTS :]], axis=0)
        else:
            parts, dout = got[head, 2 * BLOCK :], got[head, BLOCK : 2 * BLOCK]
        parts = parts.astype(jnp.float32)
        norm = parts[0:1] + parts[1:2] + parts[2:3]
        probs = jnp.exp(dot(k[at, c], query, NT) * SCALE - norm)
        grads = (probs * dot(v[at, c], dout, NT)).astype(jnp.bfloat16)
        dk[at, c] += jnp.where(active, dot(grads, query, NN), 0.0)
        dv[at, c] += jnp.where(active, dot(probs.astype(jnp.bfloat16), dout, NN), 0.0)


def most_kernel(offsets, gain, scaled, k, v, d, norm, dq_in, added, *refs):
    received, (grad_q, dk, dv, dq) = dict(zip(SOON, refs)), refs[len(SOON) :]
    for head in range(HEADS):
        c = cols(head)
        count = block_counts(offsets, head)
        query, key, value, dout = scaled[:, c], k[:, c], v[:, c], d[:, c]
        probs = jnp.exp(dot(key, query, NT) * SCALE - norm[head : head + 1, :])
        grads = (probs * dot(value, dout, NT)).astype(jnp.bfloat16)
        probs = probs.astype(jnp.bfloat16)
        for b in range(2):
            own, other = both_blocks(b)
            dk[own, c] = count[b] * dot(grads[own, own], query[own], NN) + dot(grads[own, other], query[other], NN)
            dv[own, c] = count[b] * dot(probs[own, own], dout[own], NN) + dot(probs[own, other], dout[other], NN)
    dq[...] = dq_in[...]

    def add_queries(level, spots):
        for head in range(HEADS):
            dq[block_rows(spots[head][1]), cols(head)] += added[level - 1, head]

    for_each_level(offsets, range(1, LEVELS), add_queries)
    grad_q[...] = (dq[...] * SCALE * gain[...]).astype(jnp.bfloat16)
    for_each_level(
        offsets, SOON, lambda level, spots: add_keys(level, spots, received[level], None, gain, k, v, dk, dv)
    )


def last_kernel(offsets, gain, k, v, dk_in, dv_in, *refs):
    got, first = dict(zip(LATE, refs)), dict(zip(LATE, refs[len(LATE) :]))
    grad_k, grad_v, dk, dv = refs[2 * len(LATE) :]
    dk[...] = dk_in[...]
    dv[...] = dv_in[...]
    for_each_level(
        offsets, LATE, lambda level, spots: add_keys(level, spots, got[level], first[level], gain, k, v, dk, dv)
    )
    grad_k[...] = (dk[...] * SCALE).astype(jnp.bfloat16)
    grad_v[...] = dv[...].astype(jnp.bfloat16)


def sum_kernel(parts, total):
    total[...] = jnp.sum(parts[...], axis=0)


def call(kernel, name, outs, in_specs, scratch=(), out_specs=None, aliases=None):
    return pl.pallas_call(
        kernel,
        name=name,
        out_shape=outs,
        in_specs=in_specs,
        out_specs=out_specs or [VMEM] * len(outs),
        scratch_shapes=list(scratch),
        input_output_aliases=aliases or {},
        compiler_params=pltpu.CompilerParams(vmem_limit_bytes=32 * 1024 * 1024),
    )


def in_hbm(array):
    return pltpu.with_memory_space_constraint(array, pltpu.HBM)


def swap(payloads):
    count, got = lax.axis_size("ctx"), {}
    for level, payload in payloads.items():
        half = 1 << (level - 1)
        got[level] = lax.ppermute(payload, "ctx", [(i, i ^ half) for i in range(count)])
    return got


def body(queries, keys, values, grad_out, log_norm, offsets, q_gain):
    q, k, v, d = queries[0], keys[0], values[0], grad_out[0]
    norm = log_norm[0]
    tokens, width = q.shape
    gain = q_gain.reshape(1, width)
    f32 = functools.partial(jax.ShapeDtypeStruct, dtype=jnp.float32)
    bf16 = functools.partial(jax.ShapeDtypeStruct, dtype=jnp.bfloat16)
    many = LEVELS - 1
    *firsts, norm, gain, table, q, k, v, d = call(
        pack_kernel,
        "pack",
        [bf16((HEADS, 2 * BLOCK + (PARTS + EARLY) * (level in LATE), HD)) for level in range(1, LEVELS)]
        + [f32(norm.shape), f32(gain.shape), jax.ShapeDtypeStruct(offsets.shape, jnp.int32)]
        + [bf16((tokens, width))] * 4,
        [HBM] * 7,
        [pltpu.SMEM(offsets.shape, jnp.int32), pltpu.SemaphoreType.DMA((8,))],
    )(*map(in_hbm, (offsets, k, v, d, norm, gain, q)))
    offsets = table
    got_kv = swap({level: firsts[level - 1] for level in ORDER})
    dq, scaled, partial, *picks, s1, s2, s3, s4 = call(
        local_q_kernel,
        "local_q",
        [f32((tokens, width)), bf16((tokens, width)), f32((1, width))]
        + [bf16((3, many, HEADS, BLOCK, HD)), f32((many, HEADS, BLOCK, HD)), f32((many * HEADS, HD))]
        + [bf16((HEADS, 2 * BLOCK + (-EARLY if level in LATE else PARTS), HD)) for level in range(1, LEVELS)],
        [SMEM] + [VMEM] * 6,
    )(offsets, gain, q, k, v, d, norm)
    second = (s1, s2, s3, s4)
    got_qd = swap({level: second[level - 1] for level in SOON})
    axes = ("dp", "ctx")
    everyone = lax.axis_size(axes)
    late = [second[level - 1] for level in LATE]
    added, partial, *late = call(
        query_kernel,
        "remote_q",
        [f32((many, HEADS, BLOCK, HD)), f32((everyone, 1, width))] + [bf16(p.shape) for p in late],
        [VMEM] * 8 + [ANY] * len(late),
        (),
        [VMEM] * 2 + [ANY] * len(late),
        {8 + i: 2 + i for i in range(len(late))},
    )(*picks, partial, *(got_kv[level] for level in ORDER), *late)
    got_qd.update(swap(dict(zip(LATE, late))))
    parts = lax.all_to_all(partial, axes, 0, 0, tiled=True)
    acc = pltpu.VMEM((tokens, width), jnp.float32)
    grad_q, dk, dv = call(
        most_kernel,
        "most_kv",
        [bf16((tokens, width)), f32((tokens, width)), f32((tokens, width))],
        [SMEM] + [VMEM] * (8 + len(SOON)),
        [acc],
    )(offsets, gain, scaled, k, v, d, norm, dq, added, *(got_qd[level] for level in SOON))
    grad_k, grad_v = call(
        last_kernel, "last_kv", [bf16((tokens, width))] * 2, [SMEM] + [VMEM] * (5 + 2 * len(LATE)), [acc, acc]
    )(offsets, gain, k, v, dk, dv, *(got_qd[level] for level in LATE), *(got_kv[level] for level in LATE))
    (total,) = call(sum_kernel, "gain", [f32((1, width))], [VMEM])(parts)
    return (grad_q[None], grad_k[None], grad_v[None], total.reshape(width))


def solution(mesh):
    rows = P("dp", "ctx", None)
    in_specs = (rows, rows, rows, rows, P("dp", None, "ctx"), P(), P())
    out_specs = (rows, rows, rows, P())
    return jax.shard_map(body, mesh=mesh, in_specs=in_specs, out_specs=out_specs, check_vma=False)
```

```python
import functools

import jax
import jax.numpy as jnp
from jax import lax
from jax.experimental import pallas as pl
from jax.experimental.pallas import tpu as pltpu
from jax.sharding import PartitionSpec as P

BLOCK = 128
LEVELS = 5
HEADS = 2
HD = 128
SCALE = HD**-0.5
LOG2E = 1.4426950408889634
LATE, EARLY, PARTS = (4,), 16, 16

HBM = pl.BlockSpec(memory_space=pltpu.HBM)
ANY = pl.BlockSpec(memory_space=pl.ANY)
VMEM = pl.BlockSpec(memory_space=pltpu.VMEM)
SMEM = pl.BlockSpec(memory_space=pltpu.SMEM)
ORDER = (4,1,2,3)
SOON = (3,2,1,)
NT = (((1,), (1,)), ((), ()))
TN = (((0,), (0,)), ((), ()))
NN = (((1,), (0,)), ((), ()))


def dot(left, right, dims):
    return lax.dot_general(left, right, dims, preferred_element_type=jnp.float32)


def cols(head):
    return slice(head * HD, (head + 1) * HD)


def place(offsets, me, head, level):
    half = 1 << (level - 1)
    shift = offsets[head, level] & (2 * half - 1)
    return (me & (half - 1)) == (shift >> 1), shift & 1


def block_rows(block):
    return pl.ds(pl.multiple_of(block * BLOCK, BLOCK), BLOCK)


def scale_rows(rows, gain):
    return (rows.astype(jnp.float32) * gain).astype(jnp.bfloat16)


def split_norm(norm, head, block):
    whole = jnp.where(block == 0, norm[head : head + 1, :BLOCK], norm[head : head + 1, BLOCK:])
    high = whole.astype(jnp.bfloat16).astype(jnp.float32)
    rest = whole - high
    mid = rest.astype(jnp.bfloat16).astype(jnp.float32)
    low = rest - mid
    row = lax.broadcasted_iota(jnp.int32, (PARTS, BLOCK), 0)
    parts = jnp.where(row == 0, high, jnp.where(row == 1, mid, jnp.where(row == 2, low, 0.0)))
    return parts.astype(jnp.bfloat16)


def pack_kernel(offsets_in, k_in, v_in, d_in, norm_in, gain_in, q_in, *refs):
    firsts, (norm, gain, table, q, k, v, d), (offsets, sems) = refs[:4], refs[4:11], refs[11:]
    copies = []
    moves = ((offsets_in, offsets), (k_in, k), (v_in, v), (d_in, d))
    moves += ((norm_in, norm), (gain_in, gain), (offsets_in, table), (q_in, q))
    for i, (source, target) in enumerate(moves):
        copies.append(pltpu.make_async_copy(source, target, sems.at[i]))
        copies[-1].start()
    for copy in copies[:3]:
        copy.wait()
    for level in sorted(range(1, LEVELS), key=LATE.count):
        if level == LATE[0]:
            for copy in copies[3:]:
                copy.wait()
        first = firsts[level - 1]
        for head in range(HEADS):
            block, c = offsets[head, level] & 1, cols(head)
            at = block_rows(block)
            first[head, :BLOCK] = k[at, c]
            first[head, BLOCK : 2 * BLOCK] = v[at, c]
            if level in LATE:
                start = pl.multiple_of(block * BLOCK, BLOCK)
                first[head, 2 * BLOCK : 2 * BLOCK + PARTS] = split_norm(norm, head, block)
                first[head, 2 * BLOCK + PARTS :] = d[pl.ds(start + BLOCK - EARLY, EARLY), c]


def pack_second(offsets, q, d, norm, seconds):
    for level in range(1, LEVELS):
        second = seconds[level - 1]
        for head in range(HEADS):
            block, c = offsets[head, level] & 1, cols(head)
            at = block_rows(block)
            second[head, :BLOCK] = q[at, c]
            if level in LATE:
                start = pl.multiple_of(block * BLOCK, BLOCK)
                second[head, BLOCK:] = d[pl.ds(start, BLOCK - EARLY), c]
            else:
                second[head, BLOCK : 2 * BLOCK] = d[at, c]
                second[head, 2 * BLOCK :] = split_norm(norm, head, block)


def block_counts(offsets, head):
    me = lax.axis_index("ctx")
    count = [jnp.float32(1.0), jnp.float32(1.0)]
    for level in range(1, LEVELS):
        active, block = place(offsets, me, head, level)
        for b in range(2):
            count[b] = count[b] + jnp.where(active & (block == b), 1.0, 0.0)
    return count


def both_blocks(b):
    return slice(b * BLOCK, (b + 1) * BLOCK), slice((1 - b) * BLOCK, (2 - b) * BLOCK)


def local_q_kernel(offsets, gain, q, k, v, d, norm, dq, scaled, partial, picked, picked_norm, taking, *seconds):
    pack_second(offsets, q, d, norm, seconds)
    me = lax.axis_index("ctx")
    row = lax.broadcasted_iota(jnp.int32, taking.shape, 0)
    flags = jnp.zeros(taking.shape, jnp.float32)
    parts = []
    for head in range(HEADS):
        c = cols(head)
        query, key = scale_rows(q[:, c], gain[:, c]), k[:, c]
        scaled[:, c] = query
        parts.append((c, key, dot(query, key, NT), dot(d[:, c], v[:, c], NT)))
    for head, (c, key, scores, pull) in enumerate(parts):
        column = jnp.transpose(jnp.broadcast_to(norm[head : head + 1, :], (BLOCK, 2 * BLOCK)))
        for level in range(1, LEVELS):
            active, block = place(offsets, me, head, level)
            at = block_rows(block)
            picked_norm[level - 1, head] = jnp.where(block == 0, column[:BLOCK], column[BLOCK:]) * LOG2E
            for i, source in enumerate((scaled, q, d)):
                picked[i, level - 1, head] = source[at, c]
            flags = jnp.where((row == HEADS * (level - 1) + head) & active, 1.0, flags)
        probs = jnp.exp(scores * SCALE - jnp.concatenate([column, column], axis=1))
        parts[head] = (c, key, (probs * pull).astype(jnp.bfloat16))
    for head, (c, key, grads) in enumerate(parts):
        count = block_counts(offsets, head)
        sums = 0.0
        for b in range(2):
            own, other = both_blocks(b)
            more = count[b] * dot(grads[own, own], key[own], NN) + dot(grads[own, other], key[other], NN)
            dq[own, c] = more
            sums = sums + jnp.sum(q[own, c].astype(jnp.float32) * more, axis=0, keepdims=True)
        partial[:, c] = sums
    taking[...] = flags


def for_each_level(offsets, levels, fn):
    me = lax.axis_index("ctx")
    for level in levels:
        spots = [place(offsets, me, head, level) for head in range(HEADS)]

        def both(level=level, spots=spots):
            fn(level, spots)

        if level == 1:
            both()
        else:
            pl.when(spots[0][0] | spots[1][0])(both)


def query_kernel(picked, picked_norm, taking, partial_in, r1, r2, r3, r4, *refs):
    added, partial = refs[len(LATE)], refs[len(LATE) + 1]
    received = dict(zip(ORDER, (r1, r2, r3, r4)))
    spots = [(level, head) for level in range(1, LEVELS) for head in range(HEADS)]
    products = []
    for level, head in spots:
        got, n = received[level], level - 1
        scores = dot(picked[0, n, head], got[head, :BLOCK], NT)
        products.append((scores, dot(picked[2, n, head], got[head, BLOCK : 2 * BLOCK], NT)))
    grads = []
    for (level, head), (scores, pull) in zip(spots, products):
        probs = jnp.exp2(scores * (SCALE * LOG2E) - picked_norm[level - 1, head])
        grads.append((probs * pull).astype(jnp.bfloat16))
    mores = [dot(grad, received[level][head, :BLOCK], NN) for (level, head), grad in zip(spots, grads)]
    sums = [partial_in[:, cols(head)] for head in range(HEADS)]
    for (level, head), more in zip(spots, mores):
        n = level - 1
        more = jnp.where(taking[HEADS * n + head : HEADS * n + head + 1, :] > 0.0, more, 0.0)
        added[n, head] = more
        sums[head] = sums[head] + jnp.sum(picked[1, n, head].astype(jnp.float32) * more, axis=0, keepdims=True)
    total = jnp.concatenate(sums, axis=1) * SCALE
    partial[...] = jnp.broadcast_to(total[None], partial.shape)


def add_keys(level, spots, got, first, gain, k, v, dk, dv):
    for head in range(HEADS):
        active, block = spots[head]
        c, at = cols(head), block_rows(block)
        query = scale_rows(got[head, :BLOCK], gain[:, c])
        if level in LATE:
            parts = first[head, 2 * BLOCK : 2 * BLOCK + PARTS]
            dout = jnp.concatenate([got[head, BLOCK:], first[head, 2 * BLOCK + PARTS :]], axis=0)
        else:
            parts, dout = got[head, 2 * BLOCK :], got[head, BLOCK : 2 * BLOCK]
        parts = parts.astype(jnp.float32)
        norm = parts[0:1] + parts[1:2] + parts[2:3]
        probs = jnp.exp(dot(k[at, c], query, NT) * SCALE - norm)
        grads = (probs * dot(v[at, c], dout, NT)).astype(jnp.bfloat16)
        dk[at, c] += jnp.where(active, dot(grads, query, NN), 0.0)
        dv[at, c] += jnp.where(active, dot(probs.astype(jnp.bfloat16), dout, NN), 0.0)


def most_kernel(offsets, gain, scaled, k, v, d, norm, dq_in, added, *refs):
    received, (grad_q, dk, dv, dq) = dict(zip(SOON, refs)), refs[len(SOON) :]
    for head in range(HEADS):
        c = cols(head)
        count = block_counts(offsets, head)
        query, key, value, dout = scaled[:, c], k[:, c], v[:, c], d[:, c]
        probs = jnp.exp(dot(key, query, NT) * SCALE - norm[head : head + 1, :])
        grads = (probs * dot(value, dout, NT)).astype(jnp.bfloat16)
        probs = probs.astype(jnp.bfloat16)
        for b in range(2):
            own, other = both_blocks(b)
            dk[own, c] = count[b] * dot(grads[own, own], query[own], NN) + dot(grads[own, other], query[other], NN)
            dv[own, c] = count[b] * dot(probs[own, own], dout[own], NN) + dot(probs[own, other], dout[other], NN)
    dq[...] = dq_in[...]

    def add_queries(level, spots):
        for head in range(HEADS):
            dq[block_rows(spots[head][1]), cols(head)] += added[level - 1, head]

    for_each_level(offsets, range(1, LEVELS), add_queries)
    grad_q[...] = (dq[...] * SCALE * gain[...]).astype(jnp.bfloat16)
    for_each_level(
        offsets, SOON, lambda level, spots: add_keys(level, spots, received[level], None, gain, k, v, dk, dv)
    )


def last_kernel(offsets, gain, k, v, dk_in, dv_in, *refs):
    got, first = dict(zip(LATE, refs)), dict(zip(LATE, refs[len(LATE) :]))
    grad_k, grad_v, dk, dv = refs[2 * len(LATE) :]
    dk[...] = dk_in[...]
    dv[...] = dv_in[...]
    for_each_level(
        offsets, LATE, lambda level, spots: add_keys(level, spots, got[level], first[level], gain, k, v, dk, dv)
    )
    grad_k[...] = (dk[...] * SCALE).astype(jnp.bfloat16)
    grad_v[...] = dv[...].astype(jnp.bfloat16)


def sum_kernel(parts, total):
    total[...] = jnp.sum(parts[...], axis=0)


def call(kernel, name, outs, in_specs, scratch=(), out_specs=None, aliases=None):
    return pl.pallas_call(
        kernel,
        name=name,
        out_shape=outs,
        in_specs=in_specs,
        out_specs=out_specs or [VMEM] * len(outs),
        scratch_shapes=list(scratch),
        input_output_aliases=aliases or {},
        compiler_params=pltpu.CompilerParams(vmem_limit_bytes=32 * 1024 * 1024),
    )


def in_hbm(array):
    return pltpu.with_memory_space_constraint(array, pltpu.HBM)


def swap(payloads):
    count, got = lax.axis_size("ctx"), {}
    for level, payload in payloads.items():
        half = 1 << (level - 1)
        got[level] = lax.ppermute(payload, "ctx", [(i, i ^ half) for i in range(count)])
    return got


def body(queries, keys, values, grad_out, log_norm, offsets, q_gain):
    q, k, v, d = queries[0], keys[0], values[0], grad_out[0]
    norm = log_norm[0]
    tokens, width = q.shape
    gain = q_gain.reshape(1, width)
    f32 = functools.partial(jax.ShapeDtypeStruct, dtype=jnp.float32)
    bf16 = functools.partial(jax.ShapeDtypeStruct, dtype=jnp.bfloat16)
    many = LEVELS - 1
    *firsts, norm, gain, table, q, k, v, d = call(
        pack_kernel,
        "pack",
        [bf16((HEADS, 2 * BLOCK + (PARTS + EARLY) * (level in LATE), HD)) for level in range(1, LEVELS)]
        + [f32(norm.shape), f32(gain.shape), jax.ShapeDtypeStruct(offsets.shape, jnp.int32)]
        + [bf16((tokens, width))] * 4,
        [HBM] * 7,
        [pltpu.SMEM(offsets.shape, jnp.int32), pltpu.SemaphoreType.DMA((8,))],
    )(*map(in_hbm, (offsets, k, v, d, norm, gain, q)))
    offsets = table
    got_kv = swap({level: firsts[level - 1] for level in ORDER})
    dq, scaled, partial, *picks, s1, s2, s3, s4 = call(
        local_q_kernel,
        "local_q",
        [f32((tokens, width)), bf16((tokens, width)), f32((1, width))]
        + [bf16((3, many, HEADS, BLOCK, HD)), f32((many, HEADS, BLOCK, HD)), f32((many * HEADS, HD))]
        + [bf16((HEADS, 2 * BLOCK + (-EARLY if level in LATE else PARTS), HD)) for level in range(1, LEVELS)],
        [SMEM] + [VMEM] * 6,
    )(offsets, gain, q, k, v, d, norm)
    second = (s1, s2, s3, s4)
    got_qd = swap({level: second[level - 1] for level in SOON})
    axes = ("dp", "ctx")
    everyone = lax.axis_size(axes)
    late = [second[level - 1] for level in LATE]
    added, partial, *late = call(
        query_kernel,
        "remote_q",
        [f32((many, HEADS, BLOCK, HD)), f32((everyone, 1, width))] + [bf16(p.shape) for p in late],
        [VMEM] * 8 + [ANY] * len(late),
        (),
        [VMEM] * 2 + [ANY] * len(late),
        {8 + i: 2 + i for i in range(len(late))},
    )(*picks, partial, *(got_kv[level] for level in ORDER), *late)
    got_qd.update(swap(dict(zip(LATE, late))))
    parts = lax.all_to_all(partial, axes, 0, 0, tiled=True)
    acc = pltpu.VMEM((tokens, width), jnp.float32)
    grad_q, dk, dv = call(
        most_kernel,
        "most_kv",
        [bf16((tokens, width)), f32((tokens, width)), f32((tokens, width))],
        [SMEM] + [VMEM] * (8 + len(SOON)),
        [acc],
    )(offsets, gain, scaled, k, v, d, norm, dq, added, *(got_qd[level] for level in SOON))
    grad_k, grad_v = call(
        last_kernel, "last_kv", [bf16((tokens, width))] * 2, [SMEM] + [VMEM] * (5 + 2 * len(LATE)), [acc, acc]
    )(offsets, gain, k, v, dk, dv, *(got_qd[level] for level in LATE), *(got_kv[level] for level in LATE))
    (total,) = call(sum_kernel, "gain", [f32((1, width))], [VMEM])(parts)
    return (grad_q[None], grad_k[None], grad_v[None], total.reshape(width))


def solution(mesh):
    rows = P("dp", "ctx", None)
    in_specs = (rows, rows, rows, rows, P("dp", None, "ctx"), P(), P())
    out_specs = (rows, rows, rows, P())
    return jax.shard_map(body, mesh=mesh, in_specs=in_specs, out_specs=out_specs, check_vma=False)
```
